128 devices in a mesh: rows: 8 (over y, core), cols: 16 (over x, z).
Axes of the slice: x: 4, y: 4, z: 4, core: 2. Of those that a mesh axis runs over, the one named last changes fastest.
Arguments:
- query_cells: bfloat16 [128, 1024, 1024], P('rows', 'cols'), may hold values from -6 to 6
- key_cells: bfloat16 [128, 1024, 1024], P('rows', 'cols'), may hold values from -6 to 6
- value_cells: bfloat16 [128, 1024, 1024], P('rows', 'cols'), may hold values from -6 to 6
- out_weight: bfloat16 [1024, 4096], P(None, ('rows', 'cols')), may hold values from -0.1875 to 0.1875
- row_pattern: int32 [128, 32, 6], P('rows'), may hold values from 0 to 31, as said below
- row_count: int32 [128], P('rows'), may hold values from 256 to 1024, as said below
- col_pattern: int32 [1024, 4, 2], P('cols'), may hold values from 0 to 3, as said below
- col_count: int32 [1024], P('cols'), may hold values from 32 to 128, as said below
Outputs:
- mixed: bfloat16 [128, 1024, 4096], P('rows', 'cols')
The draws below stay inside these ranges and needn't reach their ends.
Inputs may be any that keep to these rules, and one draw needn't show every extreme that they name: `row_pattern`: for each table row and query block, entry 0 is the query block itself and the 6 entries are distinct block numbers. `col_pattern`: for each table column and query block, entry 0 is the query block itself and the 2 entries are distinct block numbers. Cells of table row i at column positions row_count[i] or more are padding. Cells of table column j at row positions col_count[j] or more are padding.
All inputs are finite; a program needn't handle non-finite values.
Results may differ from the reference program's by a relative error of at most 0.006.
Values may be sent and summed in bfloat16 or wider, within the bound.
No kernel may reach another device: no remote copies, remote signals or barrier semaphores. Data moves between devices by JAX's collectives and lax.ppermute only.
A program may use at most 192 MiB of HBM per device.

```python
import jax
import jax.numpy as jnp
from jax import lax

D = 4096
HR = 4
HC = 4
HD = 128
BLK = 32
RSEL = 6
CSEL = 2
NR = 128
NC = 1024
NRB = 32
NCB = 4
HW = 1024


def draw_query_cells(key, part):
    shape_all = (NR, NC, (HR + HC) * HD)
    noise_key = jax.random.fold_in(key, 1)
    samples = jnp.clip(1.5 * jax.random.normal(noise_key, shape_all, jnp.float32), -6.0, 6.0)
    return samples.astype(jnp.bfloat16)


def draw_key_cells(key, part):
    shape_all = (NR, NC, (HR + HC) * HD)
    noise_key = jax.random.fold_in(key, 2)
    samples = jnp.clip(jax.random.normal(noise_key, shape_all, jnp.float32), -6.0, 6.0)
    return samples.astype(jnp.bfloat16)


def draw_pattern(key, line_total, blocks, chosen):
    scores = jax.random.randint(jax.random.fold_in(key, 11), (line_total, blocks, blocks - 1), 0, 1 << 20) * (blocks - 1) + jnp.arange(blocks - 1)
    ranking = jnp.argsort(scores, axis=-1)
    others = (jnp.arange(blocks)[None, :, None] + 1 + ranking[:, :, :chosen - 1]) % blocks
    own_block = jnp.broadcast_to(jnp.arange(blocks)[None, :, None], (line_total, blocks, 1))
    return jnp.concatenate([own_block, others], axis=-1).astype(jnp.int32)


def draw_counts(key, line_total, length):
    lowest = length // 4
    counts = jax.random.randint(jax.random.fold_in(key, 3), (line_total,), lowest, length + 1)
    longest = jax.random.randint(jax.random.fold_in(key, 4), (), 0, line_total)
    shortest = (longest + 1 + jax.random.randint(jax.random.fold_in(key, 5), (), 0, line_total - 1)) % line_total
    line_ids = jnp.arange(line_total)
    counts = jnp.where(line_ids == longest, length, counts)
    counts = jnp.where(line_ids == shortest, lowest, counts)
    return counts.astype(jnp.int32)


def draw_row_pattern(key, part):
    return draw_pattern(jax.random.fold_in(key, 101), NR, NRB, RSEL)


def draw_col_pattern(key, part):
    return draw_pattern(jax.random.fold_in(key, 202), NC, NCB, CSEL)


def draw_row_count(key, part):
    return draw_counts(jax.random.fold_in(key, 303), NR, NC)


def draw_col_count(key, part):
    return draw_counts(jax.random.fold_in(key, 404), NC, NR)


def block_levels(rng, extent, pieces, low, largest):
    def one(dim, blocks):
        heights = jax.random.uniform(jax.random.fold_in(jax.random.fold_in(rng, 6), dim), (blocks,), jnp.float32, low / len(pieces), largest / len(pieces))
        return jnp.repeat(jnp.exp(heights), extent[dim] // blocks).reshape((-1,) + (1,) * (len(extent) - dim - 1))

    gain = one(*pieces[0])
    for cut in pieces[1:]:
        gain = gain * one(*cut)
    return gain


def centred(rng, dims, deviation, most, cuts=(), held_as=jnp.bfloat16):
    entries = deviation * jax.random.normal(rng, dims, jnp.float32)
    if cuts:
        entries = entries * block_levels(rng, dims, cuts, -0.22, 0.18)
    return jnp.clip(entries, -most, most).astype(held_as)


def setup_inputs(seed: int = 0) -> dict:
    keys = jax.random.split(jax.random.key(seed), 9)
    return {
        "query_cells": draw_query_cells(jax.random.fold_in(keys[8], 71), 0),
        "key_cells": draw_key_cells(jax.random.fold_in(keys[8], 71), 0),
        "value_cells": centred(keys[2], (NR, NC, HW), 1.0, 6.0, ((0, 8), (1, 16))),
        "out_weight": centred(keys[3], (HW, D), HW ** -0.5, 0.1875, ((1, 128),)),
        "row_pattern": draw_row_pattern(jax.random.fold_in(keys[8], 71), 0),
        "row_count": draw_row_count(jax.random.fold_in(keys[8], 71), 0),
        "col_pattern": draw_col_pattern(jax.random.fold_in(keys[8], 71), 0),
        "col_count": draw_col_count(jax.random.fold_in(keys[8], 71), 0),
    }


NEG_FILL = -1.0e30


def block_table(pattern, blocks):
    matches = pattern[:, :, :, None] == jnp.arange(blocks, dtype=jnp.int32)[None, None, None, :]
    return jnp.any(matches, axis=2).astype(jnp.float32)


def line_attention(operands):
    queries, keys_line, values_line, allowed, line_count = operands
    positions = jnp.arange(queries.shape[0], dtype=jnp.int32)
    blocks = allowed.shape[0]
    member = ((positions // BLK)[:, None] == jnp.arange(blocks, dtype=jnp.int32)[None, :]).astype(jnp.float32)
    pair_table = jnp.dot(jnp.dot(member, allowed, precision=lax.Precision.HIGHEST), member.T, precision=lax.Precision.HIGHEST)
    key_live = (pair_table > 0.5) & (positions[None, :] < line_count)
    scores = jnp.einsum("phd,khd->hpk", queries.astype(jnp.float32), keys_line.astype(jnp.float32), precision=lax.Precision.HIGHEST) * (HD ** -0.5)
    line_max = jnp.max(jnp.where(key_live[None], scores, NEG_FILL), axis=-1)
    weights = jnp.where(key_live[None], jnp.exp(scores - line_max[:, :, None]), 0.0)
    denominator = jnp.sum(weights, axis=-1)
    query_live = positions < line_count
    rounded = weights.astype(jnp.bfloat16).astype(jnp.float32)
    attended = jnp.einsum("hpk,khd->phd", rounded, values_line.astype(jnp.float32), precision=lax.Precision.HIGHEST)
    attended = attended / jnp.where(query_live[None, :], denominator, 1.0).T[:, :, None]
    return jnp.where(query_live[:, None, None], attended, 0.0).astype(jnp.bfloat16)


def reference(query_cells, key_cells, value_cells, out_weight, row_pattern, row_count, col_pattern, col_count):
    row_width = HR * HD
    row_q = query_cells[:, :, :row_width].reshape(NR, NC, HR, HD)
    row_k = key_cells[:, :, :row_width].reshape(NR, NC, HR, HD)
    row_v = value_cells[:, :, :row_width].reshape(NR, NC, HR, HD)
    row_out = lax.map(line_attention, (row_q, row_k, row_v, block_table(row_pattern, NRB), row_count))
    col_q = jnp.swapaxes(query_cells[:, :, row_width:], 0, 1).reshape(NC, NR, HC, HD)
    col_k = jnp.swapaxes(key_cells[:, :, row_width:], 0, 1).reshape(NC, NR, HC, HD)
    col_v = jnp.swapaxes(value_cells[:, :, row_width:], 0, 1).reshape(NC, NR, HC, HD)
    col_out = jnp.swapaxes(lax.map(line_attention, (col_q, col_k, col_v, block_table(col_pattern, NCB), col_count)), 0, 1)
    heads_out = jnp.concatenate([row_out.reshape(NR, NC, row_width), col_out.reshape(NR, NC, HC * HD)], axis=-1)
    projected = jnp.dot(heads_out.reshape(NR * NC, (HR + HC) * HD), out_weight, preferred_element_type=jnp.float32)
    return projected.astype(jnp.bfloat16).reshape(NR, NC, D)
```

```python
import functools

import jax
import jax.numpy as jnp
from jax import lax
from jax.experimental import pallas as pl
from jax.experimental.pallas import tpu as pltpu
from jax.sharding import PartitionSpec as P

HR = 4
HC = 4
HD = 128
BLK = 32
NEG_FILL = -1e30


def row_pack_kernel(q_ref, k_ref, v_ref, out_ref):
    width = HR * HD
    out_ref[:, :, 0:width] = q_ref[...]
    out_ref[:, :, width : 2 * width] = k_ref[...]
    out_ref[:, :, 2 * width : 3 * width] = v_ref[...]


def row_pack(q, k, v):
    span, cells, _ = q.shape
    width = HR * HD
    step = 4
    part = pl.BlockSpec((step, cells, width), lambda i: (i, 0, 0))
    return pl.pallas_call(
        row_pack_kernel,
        grid=(span // step,),
        in_specs=[part, part, part],
        out_specs=pl.BlockSpec((step, cells, 3 * width), lambda i: (i, 0, 0)),
        out_shape=jax.ShapeDtypeStruct((span, cells, 3 * width), q.dtype),
        name="row_pack",
    )(q, k, v)


def swap_lead(x):
    return jnp.swapaxes(x.astype(jnp.float32), 0, 1).astype(jnp.bfloat16)


def col_pack_kernel(me_ref, q_ref, k_ref, v_ref, *rest):
    outs, (buf, sem) = rest[:-2], rest[-2:]
    peers = len(outs)
    width = HC * HD
    step = pl.program_id(0)
    slot = lax.rem(step, 2)

    @pl.when(step >= 2)
    def _():
        pltpu.make_async_copy(buf.at[slot], outs[0], sem.at[slot]).wait()

    for t, ref in enumerate((q_ref, k_ref, v_ref)):
        buf[slot, :, :, t * width : (t + 1) * width] = swap_lead(ref[...])
    for s in range(peers):

        @pl.when(step == s)
        def _(s=s):
            pltpu.make_async_copy(buf.at[slot], outs[s], sem.at[slot]).start()

    @pl.when(step == peers - 1)
    def _():
        pltpu.make_async_copy(buf.at[1 - slot], outs[0], sem.at[1 - slot]).wait()
        pltpu.make_async_copy(buf.at[slot], outs[0], sem.at[slot]).wait()


def col_pack(me, q, k, v, peers):
    span, cells, channels = q.shape
    width = HC * HD
    own = cells // peers
    part = pl.BlockSpec((span, own, width), lambda s, me: (0, me[0] ^ s, 1))
    piece = (own, span, 3 * width)
    return pl.pallas_call(
        col_pack_kernel,
        grid_spec=pltpu.PrefetchScalarGridSpec(
            num_scalar_prefetch=1,
            grid=(peers,),
            in_specs=[part, part, part],
            out_specs=[pl.BlockSpec(memory_space=pl.ANY)] * peers,
            scratch_shapes=[
                pltpu.VMEM((2,) + piece, q.dtype),
                pltpu.SemaphoreType.DMA((2,)),
            ],
        ),
        out_shape=[jax.ShapeDtypeStruct(piece, q.dtype)] * peers,
        name="col_pack",
    )(me, q, k, v)


def row_attend_kernel(pattern_ref, count_ref, x_ref, out_ref, *, chosen):
    width = HR * HD
    count = count_ref[0]
    blocks = x_ref.shape[0] // BLK
    key_lane = lax.broadcasted_iota(jnp.int32, (1, chosen * BLK), 1)
    slot_of = key_lane // BLK
    in_block = key_lane - slot_of * BLK
    query_row = lax.broadcasted_iota(jnp.int32, (BLK, 1), 0)
    zero = jnp.zeros((BLK, HD), jnp.bfloat16)

    def one(n):
        at = pl.multiple_of(n * BLK, BLK)
        q = x_ref[pl.ds(at, BLK), 0:width]
        keys, values = [], []
        limit = jnp.zeros((1, chosen * BLK), jnp.int32)
        for s in range(chosen):
            b = pattern_ref[n * chosen + s]
            k_at = pl.multiple_of(b * BLK, BLK)
            keys.append(x_ref[pl.ds(k_at, BLK), width : 2 * width])
            values.append(x_ref[pl.ds(k_at, BLK), 2 * width : 3 * width])
            limit = jnp.where(slot_of == s, count - b * BLK, limit)
        keys = jnp.concatenate(keys, axis=0)
        values = jnp.concatenate(values, axis=0)
        live = in_block < limit
        spread = jnp.concatenate(
            [
                jnp.concatenate(
                    [q[:, h * HD : (h + 1) * HD] if g == h else zero for g in range(HR)], axis=1
                )
                for h in range(HR)
            ],
            axis=0,
        )
        scores = lax.dot_general(
            spread, keys, (((1,), (1,)), ((), ())), preferred_element_type=jnp.float32
        ) * HD ** (-0.5)
        top = jnp.max(jnp.where(live, scores, NEG_FILL), axis=1, keepdims=True)
        weights = jnp.where(live, jnp.exp(scores - top), 0.0)
        total = jnp.sum(weights, axis=1, keepdims=True)
        weights = weights.astype(jnp.bfloat16)
        query_live = (query_row + n * BLK) < count
        for pair in range(HR // 2):
            rows = slice(pair * 2 * BLK, (pair + 1) * 2 * BLK)
            lanes = slice(pair * 2 * HD, (pair + 1) * 2 * HD)
            added = lax.dot_general(
                weights[rows],
                values[:, lanes],
                (((1,), (0,)), ((), ())),
                preferred_element_type=jnp.float32,
            )
            for g in range(2):
                h = pair * 2 + g
                part = added[g * BLK : (g + 1) * BLK, g * HD : (g + 1) * HD]
                safe = jnp.where(query_live, total[h * BLK : (h + 1) * BLK], 1.0)
                done = jnp.where(query_live, part / safe, 0.0)
                out_ref[pl.ds(at, BLK), h * HD : (h + 1) * HD] = done.astype(jnp.bfloat16)

    def group(g, _):
        for u in range(4):
            one(g * 4 + u)
        return 0

    lax.fori_loop(0, blocks // 4, group, 0)


def row_attend(pattern, count, x):
    cells = x.shape[0]
    chosen = pattern.shape[-1]
    return pl.pallas_call(
        functools.partial(row_attend_kernel, chosen=chosen),
        grid_spec=pltpu.PrefetchScalarGridSpec(
            num_scalar_prefetch=2,
            grid=(1,),
            in_specs=[pl.BlockSpec(x.shape, lambda i, *_: (0, 0), pipeline_mode=pl.Buffered(1))],
            out_specs=pl.BlockSpec((cells, HR * HD), lambda i, *_: (0, 0)),
        ),
        out_shape=jax.ShapeDtypeStruct((cells, HR * HD), x.dtype),
        name="row_attend",
    )(pattern.reshape(-1), count, x)


def col_attend_kernel(me_ref, pattern_ref, count_ref, *rest, chosen):
    peers = (len(rest) - 2) // 2
    pieces, outs, (line, held) = rest[:peers], rest[peers : 2 * peers], rest[2 * peers :]
    width = HC * HD
    me = me_ref[0]
    j = pl.program_id(0)
    span = pieces[0].shape[1]
    cells = peers * span
    own = held.shape[0]
    first = me * own + j
    count = count_ref[first]
    for s in range(peers):
        line[pl.ds(pl.multiple_of((me ^ s) * span, span), span), :] = pieces[s][0]
    key_at = lax.broadcasted_iota(jnp.int32, (1, cells), 1)
    key_block = key_at // BLK
    query_row = lax.broadcasted_iota(jnp.int32, (cells, 1), 0)
    query_live = query_row < count
    blocks = cells // BLK
    rows = []
    for n in range(blocks):
        listed = key_block == pattern_ref[(first * blocks + n) * chosen]
        for s in range(1, chosen):
            listed = listed | (key_block == pattern_ref[(first * blocks + n) * chosen + s])
        row = jnp.where(listed & (key_at < count), 1.0, 0.0)
        rows.append(jnp.broadcast_to(row, (BLK, cells)))
    live = jnp.concatenate(rows, axis=0) > 0.5
    for h in range(HC):
        q = line[:, h * HD : (h + 1) * HD]
        k = line[:, width + h * HD : width + (h + 1) * HD]
        v = line[:, 2 * width + h * HD : 2 * width + (h + 1) * HD]
        scores = lax.dot_general(
            q, k, (((1,), (1,)), ((), ())), preferred_element_type=jnp.float32
        ) * HD ** (-0.5)
        top = jnp.max(jnp.where(live, scores, NEG_FILL), axis=1, keepdims=True)
        weights = jnp.where(live, jnp.exp(scores - top), 0.0)
        total = jnp.sum(weights, axis=1, keepdims=True)
        added = lax.dot_general(
            weights.astype(jnp.bfloat16),
            v,
            (((1,), (0,)), ((), ())),
            preferred_element_type=jnp.float32,
        )
        safe = jnp.where(query_live, total, 1.0)
        held[j, :, h * HD : (h + 1) * HD] = jnp.where(query_live, added / safe, 0.0)

    @pl.when(j == own - 1)
    def _():
        for s in range(peers):
            at = pl.multiple_of((me ^ s) * span, span)
            part = held[:, pl.ds(at, span), :]
            outs[s][...] = jnp.swapaxes(part, 0, 1).astype(jnp.bfloat16)


def col_attend(me, pattern, count, pieces):
    peers = len(pieces)
    own, span, wide = pieces[0].shape
    width = HC * HD
    chosen = pattern.shape[-1]
    result = (span, own, width)
    return pl.pallas_call(
        functools.partial(col_attend_kernel, chosen=chosen),
        grid_spec=pltpu.PrefetchScalarGridSpec(
            num_scalar_prefetch=3,
            grid=(own,),
            in_specs=[pl.BlockSpec((1, span, wide), lambda j, *_: (j, 0, 0))] * peers,
            out_specs=[pl.BlockSpec(result, lambda j, *_: (0, 0, 0))] * peers,
            scratch_shapes=[
                pltpu.VMEM((peers * span, wide), jnp.bfloat16),
                pltpu.VMEM((own, peers * span, width), jnp.float32),
            ],
        ),
        out_shape=[jax.ShapeDtypeStruct(result, jnp.bfloat16)] * peers,
        name="col_attend",
    )(me, pattern.reshape(-1), count, *pieces)


def project_kernel(me_ref, row_ref, *rest):
    pieces, (w_ref, out_ref, heads) = rest[:-3], rest[-3:]
    width = HR * HD
    span, own, _ = pieces[0].shape

    @pl.when(pl.program_id(0) == 0)
    def _():
        me = me_ref[0]
        odd = lax.rem(me, 2) == 1
        heads[:, :, 0:width] = row_ref[...]
        for s in range(0, len(pieces), 2):
            a = pieces[s][...].astype(jnp.float32)
            b = pieces[s + 1][...].astype(jnp.float32)
            both = jnp.concatenate([jnp.where(odd, b, a), jnp.where(odd, a, b)], axis=1)
            at = pl.multiple_of(((me ^ s) // 2) * 2 * own, 2 * own)
            heads[:, pl.ds(at, 2 * own), width:] = both.astype(jnp.bfloat16)

    lhs = heads[...].reshape(heads.shape[0] * heads.shape[1], heads.shape[2])
    out_ref[...] = lax.dot_general(
        lhs, w_ref[...], (((1,), (1,)), ((), ())), preferred_element_type=jnp.float32
    ).astype(jnp.bfloat16)


def project(me, row_out, pieces, weight):
    span, cells, width = row_out.shape
    outs, channels = weight.shape
    tile = 512
    whole = lambda a: pl.BlockSpec(a.shape, lambda j, *_: (0,) * a.ndim)
    return pl.pallas_call(
        project_kernel,
        grid_spec=pltpu.PrefetchScalarGridSpec(
            num_scalar_prefetch=1,
            grid=(outs // tile,),
            in_specs=[whole(row_out)]
            + [whole(p) for p in pieces]
            + [pl.BlockSpec((tile, channels), lambda j, *_: (j, 0))],
            out_specs=pl.BlockSpec((span * cells, tile), lambda j, *_: (0, j)),
            scratch_shapes=[pltpu.VMEM((span, cells, channels), jnp.bfloat16)],
        ),
        out_shape=jax.ShapeDtypeStruct((span * cells, outs), jnp.bfloat16),
        name="project",
    )(me, row_out, *pieces, weight)


def swap_pieces(pieces):
    peers = len(pieces)
    return [pieces[0]] + [
        lax.ppermute(pieces[s], "rows", [(d, d ^ s) for d in range(peers)])
        for s in range(1, peers)
    ]


def body(
    query_cells, key_cells, value_cells, out_weight, row_pattern, row_count, col_pattern, col_count
):
    row_span, col_span, channels = query_cells.shape
    peers = lax.axis_size("rows")
    row_share = row_span // lax.axis_size("cols")
    weight = lax.all_gather(out_weight.T, ("rows", "cols"), axis=0, tiled=True)
    me = lax.axis_index("rows").astype(jnp.int32).reshape(1)
    row_first = lax.axis_index("cols") * row_share
    pattern = lax.dynamic_slice_in_dim(row_pattern, row_first, row_share, 0)
    count = lax.dynamic_slice_in_dim(row_count, row_first, row_share, 0)

    packed = row_pack(query_cells, key_cells, value_cells)
    lines = lax.all_to_all(packed, "cols", 0, 0, tiled=True)
    pieces = swap_pieces(col_pack(me, query_cells, key_cells, value_cells, peers))

    row_out = row_attend(pattern, count, lines.reshape(-1, lines.shape[-1]))
    row_out = lax.all_to_all(
        row_out.reshape(row_span, col_span, -1), "cols", 0, 0, tiled=True
    )
    col_out = swap_pieces(col_attend(me, col_pattern, col_count, pieces))
    projected = project(me, row_out, col_out, weight)
    return projected.reshape(row_span, col_span, projected.shape[-1])


def solution(mesh):
    placed = (
        P("rows", "cols", None),
        P("rows", "cols", None),
        P("rows", "cols", None),
        P(None, ("rows", "cols")),
        P("rows", None, None),
        P("rows"),
        P("cols", None, None),
        P("cols"),
    )
    return jax.shard_map(
        body, mesh=mesh, in_specs=placed, out_specs=P("rows", "cols", None), check_vma=False
    )
```

```python
import functools

import jax
import jax.numpy as jnp
from jax import lax
from jax.experimental import pallas as pl
from jax.experimental.pallas import tpu as pltpu
from jax.sharding import PartitionSpec as P


HR = 4
HC = 4
HD = 128
BLK = 32
NEG_FILL = -1e30


def row_pack_kernel(q_ref, k_ref, v_ref, out_ref):
    width = HR * HD
    out_ref[:, :, 0:width] = q_ref[...]
    out_ref[:, :, width : 2 * width] = k_ref[...]
    out_ref[:, :, 2 * width : 3 * width] = v_ref[...]


def row_pack(q, k, v):
    span, cells, _ = q.shape
    width = HR * HD
    step = 4
    part = pl.BlockSpec((step, cells, width), lambda i: (i, 0, 0))
    return pl.pallas_call(
        row_pack_kernel,
        grid=(span // step,),
        in_specs=[part, part, part],
        out_specs=pl.BlockSpec((step, cells, 3 * width), lambda i: (i, 0, 0)),
        out_shape=jax.ShapeDtypeStruct((span, cells, 3 * width), q.dtype),
        name="row_pack",
    )(q, k, v)


def swap_lead(x):
    return jnp.swapaxes(x.astype(jnp.float32), 0, 1).astype(jnp.bfloat16)


def col_pack_kernel(me_ref, q_ref, k_ref, v_ref, *rest):
    outs, (buf, sem) = rest[:-2], rest[-2:]
    peers = len(outs)
    width = HC * HD
    step = pl.program_id(0)
    slot = lax.rem(step, 2)

    @pl.when(step >= 2)
    def _():
        pltpu.make_async_copy(buf.at[slot], outs[0], sem.at[slot]).wait()

    for t, ref in enumerate((q_ref, k_ref, v_ref)):
        buf[slot, :, :, t * width : (t + 1) * width] = swap_lead(ref[...])
    for s in range(peers):

        @pl.when(step == s)
        def _(s=s):
            pltpu.make_async_copy(buf.at[slot], outs[s], sem.at[slot]).start()

    @pl.when(step == peers - 1)
    def _():
        pltpu.make_async_copy(buf.at[1 - slot], outs[0], sem.at[1 - slot]).wait()
        pltpu.make_async_copy(buf.at[slot], outs[0], sem.at[slot]).wait()


def col_pack(me, q, k, v, peers):
    span, cells, _ = q.shape
    width = HC * HD
    own = cells // peers
    part = pl.BlockSpec((span, own, width), lambda s, me: (0, me[0] ^ s, 1))
    piece = (own, span, 3 * width)
    return pl.pallas_call(
        col_pack_kernel,
        grid_spec=pltpu.PrefetchScalarGridSpec(
            num_scalar_prefetch=1,
            grid=(peers,),
            in_specs=[part, part, part],
            out_specs=[pl.BlockSpec(memory_space=pl.ANY)] * peers,
            scratch_shapes=[
                pltpu.VMEM((2,) + piece, q.dtype),
                pltpu.SemaphoreType.DMA((2,)),
            ],
        ),
        out_shape=[jax.ShapeDtypeStruct(piece, q.dtype)] * peers,
        name="col_pack",
    )(me, q, k, v)


def row_attend_kernel(pattern_ref, count_ref, x_ref, out_ref, *, chosen):
    width = HR * HD
    count = count_ref[0]
    blocks = x_ref.shape[0] // BLK
    key_lane = lax.broadcasted_iota(jnp.int32, (1, chosen * BLK), 1)
    slot_of = key_lane // BLK
    in_block = key_lane - slot_of * BLK
    query_row = lax.broadcasted_iota(jnp.int32, (BLK, 1), 0)
    zero = jnp.zeros((BLK, HD), jnp.bfloat16)

    def one(n):
        at = pl.multiple_of(n * BLK, BLK)
        q = x_ref[pl.ds(at, BLK), 0:width]
        keys, values = [], []
        limit = jnp.zeros((1, chosen * BLK), jnp.int32)
        for s in range(chosen):
            b = pattern_ref[n * chosen + s]
            k_at = pl.multiple_of(b * BLK, BLK)
            keys.append(x_ref[pl.ds(k_at, BLK), width : 2 * width])
            values.append(x_ref[pl.ds(k_at, BLK), 2 * width : 3 * width])
            limit = jnp.where(slot_of == s, count - b * BLK, limit)
        keys = jnp.concatenate(keys, axis=0)
        values = jnp.concatenate(values, axis=0)
        live = in_block < limit
        spread = jnp.concatenate(
            [
                jnp.concatenate(
                    [q[:, h * HD : (h + 1) * HD] if g == h else zero for g in range(HR)], axis=1
                )
                for h in range(HR)
            ],
            axis=0,
        )
        scores = lax.dot_general(
            spread, keys, (((1,), (1,)), ((), ())), preferred_element_type=jnp.float32
        ) * HD ** (-0.5)
        top = jnp.max(jnp.where(live, scores, NEG_FILL), axis=1, keepdims=True)
        weights = jnp.where(live, jnp.exp(scores - top), 0.0)
        total = jnp.sum(weights, axis=1, keepdims=True)
        weights = weights.astype(jnp.bfloat16)
        query_live = (query_row + n * BLK) < count
        for pair in range(HR // 2):
            rows = slice(pair * 2 * BLK, (pair + 1) * 2 * BLK)
            lanes = slice(pair * 2 * HD, (pair + 1) * 2 * HD)
            added = lax.dot_general(
                weights[rows],
                values[:, lanes],
                (((1,), (0,)), ((), ())),
                preferred_element_type=jnp.float32,
            )
            for g in range(2):
                h = pair * 2 + g
                part = added[g * BLK : (g + 1) * BLK, g * HD : (g + 1) * HD]
                safe = jnp.where(query_live, total[h * BLK : (h + 1) * BLK], 1.0)
                done = jnp.where(query_live, part / safe, 0.0)
                out_ref[pl.ds(at, BLK), h * HD : (h + 1) * HD] = done.astype(jnp.bfloat16)

    def group(g, _):
        for u in range(4):
            one(g * 4 + u)
        return 0

    lax.fori_loop(0, blocks // 4, group, 0)


def row_attend(pattern, count, x):
    cells = x.shape[0]
    chosen = pattern.shape[-1]
    return pl.pallas_call(
        functools.partial(row_attend_kernel, chosen=chosen),
        grid_spec=pltpu.PrefetchScalarGridSpec(
            num_scalar_prefetch=2,
            grid=(1,),
            in_specs=[pl.BlockSpec(x.shape, lambda i, *_: (0, 0), pipeline_mode=pl.Buffered(1))],
            out_specs=pl.BlockSpec((cells, HR * HD), lambda i, *_: (0, 0)),
        ),
        out_shape=jax.ShapeDtypeStruct((cells, HR * HD), x.dtype),
        name="row_attend",
    )(pattern.reshape(-1), count, x)


def col_attend_kernel(me_ref, pattern_ref, count_ref, *rest, chosen):
    peers = (len(rest) - 2) // 2
    pieces, outs, (line, held) = rest[:peers], rest[peers : 2 * peers], rest[2 * peers :]
    width = HC * HD
    me = me_ref[0]
    j = pl.program_id(0)
    span = pieces[0].shape[1]
    cells = peers * span
    own = held.shape[0]
    first = me * own + j
    count = count_ref[first]
    for s in range(peers):
        line[pl.ds(pl.multiple_of((me ^ s) * span, span), span), :] = pieces[s][0]
    key_at = lax.broadcasted_iota(jnp.int32, (1, cells), 1)
    key_block = key_at // BLK
    query_row = lax.broadcasted_iota(jnp.int32, (cells, 1), 0)
    query_live = query_row < count
    blocks = cells // BLK
    rows = []
    for n in range(blocks):
        listed = key_block == pattern_ref[(first * blocks + n) * chosen]
        for s in range(1, chosen):
            listed = listed | (key_block == pattern_ref[(first * blocks + n) * chosen + s])
        row = jnp.where(listed & (key_at < count), 1.0, 0.0)
        rows.append(jnp.broadcast_to(row, (BLK, cells)))
    live = jnp.concatenate(rows, axis=0) > 0.5
    for h in range(HC):
        q = line[:, h * HD : (h + 1) * HD]
        k = line[:, width + h * HD : width + (h + 1) * HD]
        v = line[:, 2 * width + h * HD : 2 * width + (h + 1) * HD]
        scores = lax.dot_general(
            q, k, (((1,), (1,)), ((), ())), preferred_element_type=jnp.float32
        ) * HD ** (-0.5)
        top = jnp.max(jnp.where(live, scores, NEG_FILL), axis=1, keepdims=True)
        weights = jnp.where(live, jnp.exp(scores - top), 0.0)
        total = jnp.sum(weights, axis=1, keepdims=True)
        added = lax.dot_general(
            weights.astype(jnp.bfloat16),
            v,
            (((1,), (0,)), ((), ())),
            preferred_element_type=jnp.float32,
        )
        safe = jnp.where(query_live, total, 1.0)
        held[j, :, h * HD : (h + 1) * HD] = jnp.where(query_live, added / safe, 0.0)

    @pl.when(j == own - 1)
    def _():
        for s in range(peers):
            at = pl.multiple_of((me ^ s) * span, span)
            part = held[:, pl.ds(at, span), :]
            outs[s][...] = jnp.swapaxes(part, 0, 1).astype(jnp.bfloat16)


def col_attend(me, pattern, count, pieces):
    peers = len(pieces)
    own, span, wide = pieces[0].shape
    width = HC * HD
    chosen = pattern.shape[-1]
    result = (span, own, width)
    return pl.pallas_call(
        functools.partial(col_attend_kernel, chosen=chosen),
        grid_spec=pltpu.PrefetchScalarGridSpec(
            num_scalar_prefetch=3,
            grid=(own,),
            in_specs=[pl.BlockSpec((1, span, wide), lambda j, *_: (j, 0, 0))] * peers,
            out_specs=[pl.BlockSpec(result, lambda j, *_: (0, 0, 0))] * peers,
            scratch_shapes=[
                pltpu.VMEM((peers * span, wide), jnp.bfloat16),
                pltpu.VMEM((own, peers * span, width), jnp.float32),
            ],
        ),
        out_shape=[jax.ShapeDtypeStruct(result, jnp.bfloat16)] * peers,
        name="col_attend",
    )(me, pattern.reshape(-1), count, *pieces)


def project_kernel(me_ref, row_ref, *rest):
    pieces, (w_ref, out_ref, heads) = rest[:-3], rest[-3:]
    width = HR * HD
    _, own, _ = pieces[0].shape

    @pl.when(pl.program_id(0) == 0)
    def _():
        me = me_ref[0]
        odd = lax.rem(me, 2) == 1
        heads[:, :, 0:width] = row_ref[...]
        for s in range(0, len(pieces), 2):
            a = pieces[s][...].astype(jnp.float32)
            b = pieces[s + 1][...].astype(jnp.float32)
            both = jnp.concatenate([jnp.where(odd, b, a), jnp.where(odd, a, b)], axis=1)
            at = pl.multiple_of(((me ^ s) // 2) * 2 * own, 2 * own)
            heads[:, pl.ds(at, 2 * own), width:] = both.astype(jnp.bfloat16)

    lhs = heads[...].reshape(heads.shape[0] * heads.shape[1], heads.shape[2])
    out_ref[...] = lax.dot_general(
        lhs, w_ref[...], (((1,), (1,)), ((), ())), preferred_element_type=jnp.float32
    ).astype(jnp.bfloat16)


def project(me, row_out, pieces, weight):
    span, cells, _ = row_out.shape
    outs, channels = weight.shape
    tile = 512
    whole = lambda a: pl.BlockSpec(a.shape, lambda j, *_: (0,) * a.ndim)
    return pl.pallas_call(
        project_kernel,
        grid_spec=pltpu.PrefetchScalarGridSpec(
            num_scalar_prefetch=1,
            grid=(outs // tile,),
            in_specs=[whole(row_out)]
            + [whole(p) for p in pieces]
            + [pl.BlockSpec((tile, channels), lambda j, *_: (j, 0))],
            out_specs=pl.BlockSpec((span * cells, tile), lambda j, *_: (0, j)),
            scratch_shapes=[pltpu.VMEM((span, cells, channels), jnp.bfloat16)],
        ),
        out_shape=jax.ShapeDtypeStruct((span * cells, outs), jnp.bfloat16),
        name="project",
    )(me, row_out, *pieces, weight)


def swap_pieces(pieces):
    peers = len(pieces)
    return [pieces[0]] + [
        lax.ppermute(pieces[s], "rows", [(d, d ^ s) for d in range(peers)])
        for s in range(1, peers)
    ]


def body(
    query_cells, key_cells, value_cells, out_weight, row_pattern, row_count, col_pattern, col_count
):
    row_span, col_span, _ = query_cells.shape
    peers = lax.axis_size("rows")
    row_share = row_span // lax.axis_size("cols")
    weight = lax.all_gather(out_weight.T, ("rows", "cols"), axis=0, tiled=True)
    me = lax.axis_index("rows").astype(jnp.int32).reshape(1)
    row_first = lax.axis_index("cols") * row_share
    pattern = lax.dynamic_slice_in_dim(row_pattern, row_first, row_share, 0)
    count = lax.dynamic_slice_in_dim(row_count, row_first, row_share, 0)

    packed = row_pack(query_cells, key_cells, value_cells)
    lines = lax.all_to_all(packed, "cols", 0, 0, tiled=True)
    sent = col_pack(me, query_cells, key_cells, value_cells, peers)
    pieces = swap_pieces(sent)
    row_out = row_attend(pattern, count, lines.reshape(-1, lines.shape[-1]))
    row_out = lax.all_to_all(row_out.reshape(row_span, col_span, -1), "cols", 0, 0, tiled=True)
    col_out = col_attend(me, col_pattern, col_count, pieces)
    col_out = swap_pieces(col_out)
    projected = project(me, row_out, col_out, weight)
    return projected.reshape(row_span, col_span, projected.shape[-1])


def solution(mesh):
    placed = (
        P("rows", "cols", None),
        P("rows", "cols", None),
        P("rows", "cols", None),
        P(None, ("rows", "cols")),
        P("rows", None, None),
        P("rows"),
        P("cols", None, None),
        P("cols"),
    )
    return jax.shard_map(
        body, mesh=mesh, in_specs=placed, out_specs=P("rows", "cols", None), check_vma=False
    )
```

```python
import functools
import math

import jax
import jax.numpy as jnp
from jax import lax
from jax.experimental import pallas as pl
from jax.experimental.pallas import tpu as pltpu
from jax.sharding import PartitionSpec as P


HR = 4
HC = 4
HD = 128
BLK = 32
NEG_FILL = -1e30
UNROLL = 4
EXP_SCALE = HD ** (-0.5) * math.log2(math.e)


def row_pack_kernel(q_ref, k_ref, v_ref, out_ref):
    width = HR * HD
    out_ref[:, :, 0:width] = q_ref[...]
    out_ref[:, :, width : 2 * width] = k_ref[...]
    out_ref[:, :, 2 * width : 3 * width] = v_ref[...]


def row_pack(q, k, v):
    span, cells, _ = q.shape
    width = HR * HD
    step = 4
    part = pl.BlockSpec((step, cells, width), lambda i: (i, 0, 0))
    return pl.pallas_call(
        row_pack_kernel,
        grid=(span // step,),
        in_specs=[part, part, part],
        out_specs=pl.BlockSpec((step, cells, 3 * width), lambda i: (i, 0, 0)),
        out_shape=jax.ShapeDtypeStruct((span, cells, 3 * width), q.dtype),
        name="row_pack",
    )(q, k, v)


def col_pack_kernel(me_ref, q_ref, k_ref, v_ref, *rest):
    outs, (wide, buf, sem) = rest[:-3], rest[-3:]
    peers = len(outs)
    width = HC * HD
    span, own, _ = q_ref.shape
    step = pl.program_id(0)
    slot = lax.rem(step, 2)

    @pl.when(step >= 2)
    def _():
        pltpu.make_async_copy(buf.at[slot], outs[0], sem.at[slot]).wait()

    for t, ref in enumerate((q_ref, k_ref, v_ref)):
        for h in range(HC):
            lanes = slice(h * HD, (h + 1) * HD)
            wide[t * HC + h] = ref[:, :, lanes].reshape(span * own, HD).astype(jnp.float32)
    for t in range(3):
        for h in range(HC):
            for j in range(own):
                line = wide[t * HC + h, pl.ds(j, span, stride=own), :]
                at = t * width + h * HD
                buf[slot, j, :, at : at + HD] = line.astype(jnp.bfloat16)
    for s in range(peers):

        @pl.when(step == s)
        def _(s=s):
            pltpu.make_async_copy(buf.at[slot], outs[s], sem.at[slot]).start()

    @pl.when(step == peers - 1)
    def _():
        pltpu.make_async_copy(buf.at[1 - slot], outs[0], sem.at[1 - slot]).wait()
        pltpu.make_async_copy(buf.at[slot], outs[0], sem.at[slot]).wait()


def col_pack(me, q, k, v, peers):
    span, cells, _ = q.shape
    width = HC * HD
    own = cells // peers
    part = pl.BlockSpec((span, own, width), lambda s, me: (0, me[0] ^ s, 1))
    piece = (own, span, 3 * width)
    return pl.pallas_call(
        col_pack_kernel,
        grid_spec=pltpu.PrefetchScalarGridSpec(
            num_scalar_prefetch=1,
            grid=(peers,),
            in_specs=[part, part, part],
            out_specs=[pl.BlockSpec(memory_space=pl.ANY)] * peers,
            scratch_shapes=[
                pltpu.VMEM((3 * HC, span * own, HD), jnp.float32),
                pltpu.VMEM((2,) + piece, q.dtype),
                pltpu.SemaphoreType.DMA((2,)),
            ],
        ),
        out_shape=[jax.ShapeDtypeStruct(piece, q.dtype)] * peers,
        name="col_pack",
    )(me, q, k, v)


def row_attend_kernel(pattern_ref, count_ref, x_ref, out_ref, *, chosen):
    width = HR * HD
    count = count_ref[0]
    blocks = x_ref.shape[0] // BLK
    key_lane = lax.broadcasted_iota(jnp.int32, (1, chosen * BLK), 1)
    slot_of = key_lane // BLK
    in_block = key_lane - slot_of * BLK
    query_row = lax.broadcasted_iota(jnp.int32, (BLK, 1), 0)
    zero = jnp.zeros((BLK, HD), jnp.bfloat16)

    def stage_scores(n):
        at = pl.multiple_of(n * BLK, BLK)
        q = x_ref[pl.ds(at, BLK), 0:width]
        keys = []
        limit = jnp.zeros((1, chosen * BLK), jnp.int32)
        for s in range(chosen):
            b = pattern_ref[n * chosen + s]
            k_at = pl.multiple_of(b * BLK, BLK)
            keys.append(x_ref[pl.ds(k_at, BLK), width : 2 * width])
            limit = jnp.where(slot_of == s, count - b * BLK, limit)
        keys = jnp.concatenate(keys, axis=0)
        live = in_block < limit
        spread = jnp.concatenate(
            [
                jnp.concatenate(
                    [q[:, h * HD : (h + 1) * HD] if g == h else zero for g in range(HR)], axis=1
                )
                for h in range(HR)
            ],
            axis=0,
        )
        scores = lax.dot_general(
            spread, keys, (((1,), (1,)), ((), ())), preferred_element_type=jnp.float32
        )
        return jnp.where(live, scores, NEG_FILL)

    def stage_values(n, weights, total):
        at = pl.multiple_of(n * BLK, BLK)
        values = []
        for s in range(chosen):
            k_at = pl.multiple_of(pattern_ref[n * chosen + s] * BLK, BLK)
            values.append(x_ref[pl.ds(k_at, BLK), 2 * width : 3 * width])
        values = jnp.concatenate(values, axis=0)
        query_live = (query_row + n * BLK) < count
        for pair in range(HR // 2):
            rows = slice(pair * 2 * BLK, (pair + 1) * 2 * BLK)
            lanes = slice(pair * 2 * HD, (pair + 1) * 2 * HD)
            added = lax.dot_general(
                weights[rows],
                values[:, lanes],
                (((1,), (0,)), ((), ())),
                preferred_element_type=jnp.float32,
            )
            for g in range(2):
                h = pair * 2 + g
                part = added[g * BLK : (g + 1) * BLK, g * HD : (g + 1) * HD]
                safe = jnp.where(query_live, total[h * BLK : (h + 1) * BLK], 1.0)
                done = jnp.where(query_live, part / safe, 0.0)
                out_ref[pl.ds(at, BLK), h * HD : (h + 1) * HD] = done.astype(jnp.bfloat16)

    def group(g, _):
        blocks_here = [g * UNROLL + u for u in range(UNROLL)]
        scores = [stage_scores(n) for n in blocks_here]
        tops = [jnp.max(s, axis=1, keepdims=True) for s in scores]
        weights = [jnp.exp2((s - m) * EXP_SCALE) for s, m in zip(scores, tops)]
        totals = [jnp.sum(w, axis=1, keepdims=True) for w in weights]
        for n, w, t in zip(blocks_here, weights, totals):
            stage_values(n, w.astype(jnp.bfloat16), t)
        return 0

    lax.fori_loop(0, blocks // UNROLL, group, 0)


def row_attend(pattern, count, x):
    cells = x.shape[0]
    chosen = pattern.shape[-1]
    return pl.pallas_call(
        functools.partial(row_attend_kernel, chosen=chosen),
        grid_spec=pltpu.PrefetchScalarGridSpec(
            num_scalar_prefetch=2,
            grid=(1,),
            in_specs=[pl.BlockSpec(x.shape, lambda i, *_: (0, 0), pipeline_mode=pl.Buffered(1))],
            out_specs=pl.BlockSpec((cells, HR * HD), lambda i, *_: (0, 0)),
        ),
        out_shape=jax.ShapeDtypeStruct((cells, HR * HD), x.dtype),
        name="row_attend",
    )(pattern.reshape(-1), count, x)


def col_attend_kernel(me_ref, pattern_ref, count_ref, *rest, chosen, lines):
    peers = (len(rest) - 2) // 2
    pieces, outs, (line, held) = rest[:peers], rest[peers : 2 * peers], rest[2 * peers :]
    width = HC * HD
    me = me_ref[0]
    step = pl.program_id(0)
    span = pieces[0].shape[1]
    cells = peers * span
    own = held.shape[1] // cells
    blocks = cells // BLK
    key_at = lax.broadcasted_iota(jnp.int32, (1, cells), 1)
    key_block = key_at // BLK
    query_row = lax.broadcasted_iota(jnp.int32, (cells, 1), 0)
    for u in range(lines):
        for s in range(peers):
            line[u, pl.ds(pl.multiple_of((me ^ s) * span, span), span), :] = pieces[s][u]
    jobs, scores = [], []
    for u in range(lines):
        j = step * lines + u
        first = me * own + j
        count = count_ref[first]
        rows = []
        for n in range(blocks):
            listed = key_block == pattern_ref[(first * blocks + n) * chosen]
            for s in range(1, chosen):
                listed = listed | (key_block == pattern_ref[(first * blocks + n) * chosen + s])
            row = jnp.where(listed & (key_at < count), 0.0, NEG_FILL)
            rows.append(jnp.broadcast_to(row, (BLK, cells)))
        bias = jnp.concatenate(rows, axis=0)
        query_live = query_row < count
        for h in range(HC):
            q = line[u, :, h * HD : (h + 1) * HD]
            k = line[u, :, width + h * HD : width + (h + 1) * HD]
            product = lax.dot_general(
                q, k, (((1,), (1,)), ((), ())), preferred_element_type=jnp.float32
            )
            scores.append(jnp.where(bias < 0.0, NEG_FILL, product))
            jobs.append((u, j, h, query_live))
    tops = [jnp.max(s, axis=1, keepdims=True) for s in scores]
    weights = [jnp.exp2((s - m) * EXP_SCALE) for s, m in zip(scores, tops)]
    totals = [jnp.sum(w, axis=1, keepdims=True) for w in weights]
    for (u, j, h, query_live), w, total in zip(jobs, weights, totals):
        v = line[u, :, 2 * width + h * HD : 2 * width + (h + 1) * HD]
        added = lax.dot_general(
            w.astype(jnp.bfloat16), v, (((1,), (0,)), ((), ())), preferred_element_type=jnp.float32
        )
        safe = jnp.where(query_live, total, 1.0)
        done = jnp.where(query_live, added / safe, 0.0)
        held[h, pl.ds(j, cells, stride=own), :] = done

    @pl.when(step == pl.num_programs(0) - 1)
    def _():
        for s in range(peers):
            at = pl.multiple_of((me ^ s) * span * own, span * own)
            for h in range(HC):
                part = held[h, pl.ds(at, span * own), :].reshape(span, own, HD)
                outs[s][:, :, h * HD : (h + 1) * HD] = part.astype(jnp.bfloat16)


def col_attend(me, pattern, count, pieces):
    peers = len(pieces)
    own, span, wide = pieces[0].shape
    width = HC * HD
    chosen = pattern.shape[-1]
    lines = 2
    result = (span, own, width)
    return pl.pallas_call(
        functools.partial(col_attend_kernel, chosen=chosen, lines=lines),
        grid_spec=pltpu.PrefetchScalarGridSpec(
            num_scalar_prefetch=3,
            grid=(own // lines,),
            in_specs=[pl.BlockSpec((lines, span, wide), lambda j, *_: (j, 0, 0))] * peers,
            out_specs=[pl.BlockSpec(result, lambda j, *_: (0, 0, 0))] * peers,
            scratch_shapes=[
                pltpu.VMEM((lines, peers * span, wide), jnp.bfloat16),
                pltpu.VMEM((HC, own * peers * span, HD), jnp.float32),
            ],
        ),
        out_shape=[jax.ShapeDtypeStruct(result, jnp.bfloat16)] * peers,
        name="col_attend",
    )(me, pattern.reshape(-1), count, *pieces)


def project_first_kernel(me_ref, row_ref, *rest):
    pieces, (w_ref, out_ref, heads) = rest[:-3], rest[-3:]
    width = HR * HD
    own = pieces[0].shape[1]

    @pl.when(pl.program_id(0) == 0)
    def _():
        me = me_ref[0]
        odd = lax.rem(me, 2) == 1
        heads[:, :, 0:width] = row_ref[...]
        for s in range(0, len(pieces), 2):
            a = pieces[s][...].astype(jnp.float32)
            b = pieces[s + 1][...].astype(jnp.float32)
            both = jnp.concatenate([jnp.where(odd, b, a), jnp.where(odd, a, b)], axis=1)
            at = pl.multiple_of(((me ^ s) // 2) * 2 * own, 2 * own)
            heads[:, pl.ds(at, 2 * own), width:] = both.astype(jnp.bfloat16)

    project_block(heads, w_ref, out_ref)


def project_block(heads, w_ref, out_ref):
    channels = heads.shape[2]
    out_ref[...] = lax.dot_general(
        heads[...].reshape(-1, channels),
        w_ref[...].reshape(-1, channels),
        (((1,), (1,)), ((), ())),
        preferred_element_type=jnp.float32,
    ).astype(jnp.bfloat16)


def project_second_kernel(me_ref, heads, w_ref, kept_ref, out_ref):
    project_block(heads, w_ref, out_ref)


def weight_spec(weight):
    planes, _, span, channels = weight.shape
    return pl.BlockSpec((planes, None, span, channels), lambda j, *_: (0, j, 0, 0))


def whole(a):
    return pl.BlockSpec(a.shape, lambda j, *_: (0,) * a.ndim)


def project_first(me, row_out, pieces, weight, outs):
    span, cells, _ = row_out.shape
    planes, turns, part, channels = weight.shape
    tile = planes * part
    return pl.pallas_call(
        project_first_kernel,
        grid_spec=pltpu.PrefetchScalarGridSpec(
            num_scalar_prefetch=1,
            grid=(turns,),
            in_specs=[whole(row_out)] + [whole(p) for p in pieces] + [weight_spec(weight)],
            out_specs=[
                pl.BlockSpec((span * cells, tile), lambda j, me: (0, me[0] ^ (2 * j))),
                pl.BlockSpec((span, cells, channels), lambda j, *_: (0, 0, 0)),
            ],
        ),
        out_shape=[
            jax.ShapeDtypeStruct((span * cells, outs), jnp.bfloat16),
            jax.ShapeDtypeStruct((span, cells, channels), jnp.bfloat16),
        ],
        name="project_first",
    )(me, row_out, *pieces, weight)


def project_second(me, heads, weight, kept):
    span, cells, _ = heads.shape
    planes, turns, part, _ = weight.shape
    tile = planes * part
    return pl.pallas_call(
        project_second_kernel,
        grid_spec=pltpu.PrefetchScalarGridSpec(
            num_scalar_prefetch=1,
            grid=(turns,),
            in_specs=[whole(heads), weight_spec(weight), pl.BlockSpec(memory_space=pl.ANY)],
            out_specs=pl.BlockSpec((span * cells, tile), lambda j, me: (0, me[0] ^ (2 * j + 1))),
        ),
        out_shape=jax.ShapeDtypeStruct(kept.shape, jnp.bfloat16),
        input_output_aliases={3: 0},
        name="project_second",
    )(me, heads, weight, kept)


def swap_pieces(pieces):
    peers = len(pieces)
    return [pieces[0]] + [
        lax.ppermute(pieces[s], "rows", [(d, d ^ s) for d in range(peers)])
        for s in range(1, peers)
    ]


def body(
    query_cells, key_cells, value_cells, out_weight, row_pattern, row_count, col_pattern, col_count
):
    row_span, col_span, _ = query_cells.shape
    peers = lax.axis_size("rows")
    row_share = row_span // lax.axis_size("cols")
    me = lax.axis_index("rows").astype(jnp.int32).reshape(1)
    row_first = lax.axis_index("cols") * row_share
    pattern = lax.dynamic_slice_in_dim(row_pattern, row_first, row_share, 0)
    count = lax.dynamic_slice_in_dim(row_count, row_first, row_share, 0)

    shard = out_weight.T
    near = [shard] + [
        lax.ppermute(shard, "rows", [(d, d ^ s) for d in range(peers)])
        for s in range(2, peers, 2)
    ]
    weight = lax.all_gather(jnp.stack(near)[None], "cols", axis=0, tiled=True)
    weight_other = lax.ppermute(weight, "rows", [(d, d ^ 1) for d in range(peers)])
    sent = col_pack(me, query_cells, key_cells, value_cells, peers)
    pieces = swap_pieces(sent)
    packed = row_pack(query_cells, key_cells, value_cells)
    lines = lax.all_to_all(packed, "cols", 0, 0, tiled=True)
    col_out = col_attend(me, col_pattern, col_count, pieces)
    col_out = swap_pieces(col_out)
    row_out = row_attend(pattern, count, lines.reshape(-1, lines.shape[-1]))
    row_out = lax.all_to_all(row_out.reshape(row_span, col_span, -1), "cols", 0, 0, tiled=True)
    half, heads = project_first(
        me, row_out, col_out, weight, out_weight.shape[1] * peers * lax.axis_size("cols")
    )
    projected = project_second(me, heads, weight_other, half)
    return projected.reshape(row_span, col_span, projected.shape[-1])


def solution(mesh):
    placed = (
        P("rows", "cols", None),
        P("rows", "cols", None),
        P("rows", "cols", None),
        P(None, ("rows", "cols")),
        P("rows", None, None),
        P("rows"),
        P("cols", None, None),
        P("cols"),
    )
    return jax.shard_map(
        body, mesh=mesh, in_specs=placed, out_specs=P("rows", "cols", None), check_vma=False
    )
```

```python
import functools
import math

import jax
import jax.numpy as jnp
from jax import lax
from jax.experimental import pallas as pl
from jax.experimental.pallas import tpu as pltpu
from jax.sharding import PartitionSpec as P


HR = 4
HC = 4
HD = 128
BLK = 32
NEG_FILL = -1e30
UNROLL = 4
EXP_SCALE = HD ** (-0.5) * math.log2(math.e)


def row_pack_kernel(q_ref, k_ref, v_ref, out_ref):
    width = HR * HD
    out_ref[:, :, 0:width] = q_ref[...]
    out_ref[:, :, width : 2 * width] = k_ref[...]
    out_ref[:, :, 2 * width : 3 * width] = v_ref[...]


def row_pack(q, k, v):
    span, cells, _ = q.shape
    width = HR * HD
    step = 4
    part = pl.BlockSpec((step, cells, width), lambda i: (i, 0, 0))
    return pl.pallas_call(
        row_pack_kernel,
        grid=(span // step,),
        in_specs=[part, part, part],
        out_specs=pl.BlockSpec((step, cells, 3 * width), lambda i: (i, 0, 0)),
        out_shape=jax.ShapeDtypeStruct((span, cells, 3 * width), q.dtype),
        name="row_pack",
    )(q, k, v)


def col_pack_kernel(me_ref, q_ref, k_ref, v_ref, *rest):
    outs, (wide, buf, sem) = rest[:-3], rest[-3:]
    peers = len(outs)
    width = HC * HD
    span, own, _ = q_ref.shape
    step = pl.program_id(0)
    slot = lax.rem(step, 2)

    @pl.when(step >= 2)
    def _():
        pltpu.make_async_copy(buf.at[slot], outs[0], sem.at[slot]).wait()

    for t, ref in enumerate((q_ref, k_ref, v_ref)):
        for h in range(HC):
            lanes = slice(h * HD, (h + 1) * HD)
            wide[t * HC + h] = ref[:, :, lanes].reshape(span * own, HD).astype(jnp.float32)
    for t in range(3):
        for h in range(HC):
            for j in range(own):
                line = wide[t * HC + h, pl.ds(j, span, stride=own), :]
                at = t * width + h * HD
                buf[slot, j, :, at : at + HD] = line.astype(jnp.bfloat16)
    for s in range(peers):

        @pl.when(step == s)
        def _(s=s):
            pltpu.make_async_copy(buf.at[slot], outs[s], sem.at[slot]).start()

    @pl.when(step == peers - 1)
    def _():
        pltpu.make_async_copy(buf.at[1 - slot], outs[0], sem.at[1 - slot]).wait()
        pltpu.make_async_copy(buf.at[slot], outs[0], sem.at[slot]).wait()


def col_pack(me, q, k, v, peers):
    span, cells, _ = q.shape
    width = HC * HD
    own = cells // peers
    part = pl.BlockSpec((span, own, width), lambda s, me: (0, me[0] ^ s, 1))
    piece = (own, span, 3 * width)
    return pl.pallas_call(
        col_pack_kernel,
        grid_spec=pltpu.PrefetchScalarGridSpec(
            num_scalar_prefetch=1,
            grid=(peers,),
            in_specs=[part, part, part],
            out_specs=[pl.BlockSpec(memory_space=pl.ANY)] * peers,
            scratch_shapes=[
                pltpu.VMEM((3 * HC, span * own, HD), jnp.float32),
                pltpu.VMEM((2,) + piece, q.dtype),
                pltpu.SemaphoreType.DMA((2,)),
            ],
        ),
        out_shape=[jax.ShapeDtypeStruct(piece, q.dtype)] * peers,
        name="col_pack",
    )(me, q, k, v)


def row_attend_kernel(pattern_ref, count_ref, x_ref, out_ref, *, chosen):
    width = HR * HD
    count = count_ref[0]
    blocks = x_ref.shape[0] // BLK
    key_lane = lax.broadcasted_iota(jnp.int32, (1, chosen * BLK), 1)
    slot_of = key_lane // BLK
    in_block = key_lane - slot_of * BLK
    query_row = lax.broadcasted_iota(jnp.int32, (BLK, 1), 0)
    zero = jnp.zeros((BLK, HD), jnp.bfloat16)

    def stage_scores(n):
        at = pl.multiple_of(n * BLK, BLK)
        q = x_ref[pl.ds(at, BLK), 0:width]
        keys = []
        limit = jnp.zeros((1, chosen * BLK), jnp.int32)
        for s in range(chosen):
            b = pattern_ref[n * chosen + s]
            k_at = pl.multiple_of(b * BLK, BLK)
            keys.append(x_ref[pl.ds(k_at, BLK), width : 2 * width])
            limit = jnp.where(slot_of == s, count - b * BLK, limit)
        keys = jnp.concatenate(keys, axis=0)
        live = in_block < limit
        spread = jnp.concatenate(
            [
                jnp.concatenate(
                    [q[:, h * HD : (h + 1) * HD] if g == h else zero for g in range(HR)], axis=1
                )
                for h in range(HR)
            ],
            axis=0,
        )
        scores = lax.dot_general(
            spread, keys, (((1,), (1,)), ((), ())), preferred_element_type=jnp.float32
        )
        return jnp.where(live, scores, NEG_FILL)

    def stage_values(n, weights, total):
        at = pl.multiple_of(n * BLK, BLK)
        values = []
        for s in range(chosen):
            k_at = pl.multiple_of(pattern_ref[n * chosen + s] * BLK, BLK)
            values.append(x_ref[pl.ds(k_at, BLK), 2 * width : 3 * width])
        values = jnp.concatenate(values, axis=0)
        query_live = (query_row + n * BLK) < count
        for pair in range(HR // 2):
            rows = slice(pair * 2 * BLK, (pair + 1) * 2 * BLK)
            lanes = slice(pair * 2 * HD, (pair + 1) * 2 * HD)
            added = lax.dot_general(
                weights[rows],
                values[:, lanes],
                (((1,), (0,)), ((), ())),
                preferred_element_type=jnp.float32,
            )
            for g in range(2):
                h = pair * 2 + g
                part = added[g * BLK : (g + 1) * BLK, g * HD : (g + 1) * HD]
                safe = jnp.where(query_live, total[h * BLK : (h + 1) * BLK], 1.0)
                done = jnp.where(query_live, part / safe, 0.0)
                out_ref[pl.ds(at, BLK), h * HD : (h + 1) * HD] = done.astype(jnp.bfloat16)

    def group(g, _):
        blocks_here = [g * UNROLL + u for u in range(UNROLL)]
        scores = [stage_scores(n) for n in blocks_here]
        tops = [jnp.max(s, axis=1, keepdims=True) for s in scores]
        weights = [jnp.exp2((s - m) * EXP_SCALE) for s, m in zip(scores, tops)]
        totals = [jnp.sum(w, axis=1, keepdims=True) for w in weights]
        for n, w, t in zip(blocks_here, weights, totals):
            stage_values(n, w.astype(jnp.bfloat16), t)
        return 0

    lax.fori_loop(0, blocks // UNROLL, group, 0)


def row_attend(pattern, count, x):
    cells = x.shape[0]
    chosen = pattern.shape[-1]
    return pl.pallas_call(
        functools.partial(row_attend_kernel, chosen=chosen),
        grid_spec=pltpu.PrefetchScalarGridSpec(
            num_scalar_prefetch=2,
            grid=(1,),
            in_specs=[pl.BlockSpec(memory_space=pltpu.VMEM)],
            out_specs=pl.BlockSpec((cells, HR * HD), lambda i, *_: (0, 0)),
        ),
        out_shape=jax.ShapeDtypeStruct((cells, HR * HD), x.dtype),
        name="row_attend",
    )(pattern.reshape(-1), count, x)


def col_attend_kernel(me_ref, pattern_ref, count_ref, *rest, chosen, lines):
    peers = (len(rest) - 2) // 2
    pieces, outs, (line, held) = rest[:peers], rest[peers : 2 * peers], rest[2 * peers :]
    width = HC * HD
    me = me_ref[0]
    step = pl.program_id(0)
    span = pieces[0].shape[1]
    cells = peers * span
    own = held.shape[1] // cells
    blocks = cells // BLK
    key_at = lax.broadcasted_iota(jnp.int32, (1, cells), 1)
    key_block = key_at // BLK
    query_row = lax.broadcasted_iota(jnp.int32, (cells, 1), 0)
    for u in range(lines):
        for s in range(peers):
            line[u, pl.ds(pl.multiple_of((me ^ s) * span, span), span), :] = pieces[s][u]
    jobs, scores = [], []
    for u in range(lines):
        j = step * lines + u
        first = me * own + j
        count = count_ref[first]
        rows = []
        for n in range(blocks):
            listed = key_block == pattern_ref[(first * blocks + n) * chosen]
            for s in range(1, chosen):
                listed = listed | (key_block == pattern_ref[(first * blocks + n) * chosen + s])
            row = jnp.where(listed & (key_at < count), 0.0, NEG_FILL)
            rows.append(jnp.broadcast_to(row, (BLK, cells)))
        bias = jnp.concatenate(rows, axis=0)
        query_live = query_row < count
        for h in range(HC):
            q = line[u, :, h * HD : (h + 1) * HD]
            k = line[u, :, width + h * HD : width + (h + 1) * HD]
            product = lax.dot_general(
                q, k, (((1,), (1,)), ((), ())), preferred_element_type=jnp.float32
            )
            scores.append(jnp.where(bias < 0.0, NEG_FILL, product))
            jobs.append((u, j, h, query_live))
    tops = [jnp.max(s, axis=1, keepdims=True) for s in scores]
    weights = [jnp.exp2((s - m) * EXP_SCALE) for s, m in zip(scores, tops)]
    totals = [jnp.sum(w, axis=1, keepdims=True) for w in weights]
    for (u, j, h, query_live), w, total in zip(jobs, weights, totals):
        v = line[u, :, 2 * width + h * HD : 2 * width + (h + 1) * HD]
        added = lax.dot_general(
            w.astype(jnp.bfloat16), v, (((1,), (0,)), ((), ())), preferred_element_type=jnp.float32
        )
        safe = jnp.where(query_live, total, 1.0)
        done = jnp.where(query_live, added / safe, 0.0)
        held[h, pl.ds(j, cells, stride=own), :] = done

    @pl.when(step == pl.num_programs(0) - 1)
    def _():
        for s in range(peers):
            at = pl.multiple_of((me ^ s) * span * own, span * own)
            for h in range(HC):
                part = held[h, pl.ds(at, span * own), :].reshape(span, own, HD)
                outs[s][:, :, h * HD : (h + 1) * HD] = part.astype(jnp.bfloat16)


def col_attend(me, pattern, count, pieces):
    peers = len(pieces)
    own, span, wide = pieces[0].shape
    width = HC * HD
    chosen = pattern.shape[-1]
    lines = 2
    result = (span, own, width)
    return pl.pallas_call(
        functools.partial(col_attend_kernel, chosen=chosen, lines=lines),
        grid_spec=pltpu.PrefetchScalarGridSpec(
            num_scalar_prefetch=3,
            grid=(own // lines,),
            in_specs=[pl.BlockSpec((lines, span, wide), lambda j, *_: (j, 0, 0))] * peers,
            out_specs=[pl.BlockSpec(result, lambda j, *_: (0, 0, 0))] * peers,
            scratch_shapes=[
                pltpu.VMEM((lines, peers * span, wide), jnp.bfloat16),
                pltpu.VMEM((HC, own * peers * span, HD), jnp.float32),
            ],
        ),
        out_shape=[jax.ShapeDtypeStruct(result, jnp.bfloat16)] * peers,
        name="col_attend",
    )(me, pattern.reshape(-1), count, *pieces)


def project_block(plane, heads, weights, line, out_ref):
    quarter = len(weights)
    near, span, channels = weights[0].shape
    for sx in range(quarter):
        for sz in range(near):
            at = ((plane // near ^ sx) * near + (lax.rem(plane, near) ^ sz)) * span
            line[pl.ds(pl.multiple_of(at, span), span), :] = weights[sx][sz]
    out_ref[...] = lax.dot_general(
        heads[...].reshape(-1, channels),
        line[...],
        (((1,), (1,)), ((), ())),
        preferred_element_type=jnp.float32,
    ).astype(jnp.bfloat16)


def project_first_kernel(me_ref, row_ref, *rest, quarter):
    pieces, weights = rest[: -3 - quarter], rest[-3 - quarter : -3]
    out_ref, heads, line = rest[-3:]
    width = HR * HD
    own = pieces[0].shape[1]

    @pl.when(pl.program_id(0) == 0)
    def _():
        me = me_ref[0]
        odd = lax.rem(me, 2) == 1
        heads[:, :, 0:width] = row_ref[...]
        for s in range(0, len(pieces), 2):
            a = pieces[s][...].astype(jnp.float32)
            b = pieces[s + 1][...].astype(jnp.float32)
            both = jnp.concatenate([jnp.where(odd, b, a), jnp.where(odd, a, b)], axis=1)
            at = pl.multiple_of(((me ^ s) // 2) * 2 * own, 2 * own)
            heads[:, pl.ds(at, 2 * own), width:] = both.astype(jnp.bfloat16)

    project_block(me_ref[1], heads, weights, line, out_ref)


def project_second_kernel(me_ref, heads, *rest, quarter):
    weights, (_, out_ref, line) = rest[:quarter], rest[quarter:]
    project_block(me_ref[1], heads, weights, line, out_ref)


def weight_spec(weight):
    near, _, span, channels = weight.shape
    return pl.BlockSpec((near, None, span, channels), lambda j, *_: (0, j, 0, 0))


def whole(a):
    return pl.BlockSpec(a.shape, lambda j, *_: (0,) * a.ndim)


def project_first(me, row_out, pieces, weights, outs):
    span, cells, _ = row_out.shape
    near, turns, part, channels = weights[0].shape
    tile = len(weights) * near * part
    held = pl.BlockSpec(memory_space=pltpu.VMEM)
    return pl.pallas_call(
        functools.partial(project_first_kernel, quarter=len(weights)),
        grid_spec=pltpu.PrefetchScalarGridSpec(
            num_scalar_prefetch=1,
            grid=(turns,),
            in_specs=[held] * (1 + len(pieces)) + [weight_spec(w) for w in weights],
            out_specs=[
                pl.BlockSpec((span * cells, tile), lambda j, me: (0, me[0] ^ (2 * j))),
                pl.BlockSpec((span, cells, channels), lambda j, *_: (0, 0, 0)),
            ],
            scratch_shapes=[pltpu.VMEM((tile, channels), jnp.bfloat16)],
        ),
        out_shape=[
            jax.ShapeDtypeStruct((span * cells, outs), jnp.bfloat16),
            jax.ShapeDtypeStruct((span, cells, channels), jnp.bfloat16),
        ],
        name="project_first",
    )(me, row_out, *pieces, *weights)


def project_second(me, heads, weights, kept):
    span, cells, channels = heads.shape
    near, turns, part, _ = weights[0].shape
    tile = len(weights) * near * part
    return pl.pallas_call(
        functools.partial(project_second_kernel, quarter=len(weights)),
        grid_spec=pltpu.PrefetchScalarGridSpec(
            num_scalar_prefetch=1,
            grid=(turns,),
            in_specs=[whole(heads)]
            + [weight_spec(w) for w in weights]
            + [pl.BlockSpec(memory_space=pl.ANY)],
            out_specs=pl.BlockSpec((span * cells, tile), lambda j, me: (0, me[0] ^ (2 * j + 1))),
            scratch_shapes=[pltpu.VMEM((tile, channels), jnp.bfloat16)],
        ),
        out_shape=jax.ShapeDtypeStruct(kept.shape, jnp.bfloat16),
        input_output_aliases={2 + len(weights): 0},
        name="project_second",
    )(me, heads, *weights, kept)


def by_xor(x, axis, masks):
    size = lax.axis_size(axis)
    return [lax.ppermute(x, axis, [(d, d ^ s) for d in range(size)]) for s in masks]


def swap_pieces(pieces):
    peers = len(pieces)
    return [pieces[0]] + [
        lax.ppermute(pieces[s], "rows", [(d, d ^ s) for d in range(peers)])
        for s in range(1, peers)
    ]


def body(
    query_cells, key_cells, value_cells, out_weight, row_pattern, row_count, col_pattern, col_count
):
    row_span, col_span, _ = query_cells.shape
    peers = lax.axis_size("rows")
    row_share = row_span // lax.axis_size("cols")
    me = lax.axis_index("rows").astype(jnp.int32).reshape(1)
    row_first = lax.axis_index("cols") * row_share
    pattern = lax.dynamic_slice_in_dim(row_pattern, row_first, row_share, 0)
    count = lax.dynamic_slice_in_dim(row_count, row_first, row_share, 0)

    place = jnp.stack([lax.axis_index("rows"), lax.axis_index("cols")]).astype(jnp.int32)

    shard = out_weight.T
    along_y = [shard] + by_xor(shard, "rows", (2, 4, 6))
    packed = row_pack(query_cells, key_cells, value_cells)
    lines = lax.all_to_all(packed, "cols", 0, 0, tiled=True)
    held = jnp.stack(along_y)
    along_z = [held] + by_xor(held, "cols", (1, 2, 3))
    sent = col_pack(me, query_cells, key_cells, value_cells, peers)
    pieces = swap_pieces(sent)
    held = jnp.stack(along_z)
    weights = [held] + by_xor(held, "cols", (4, 8, 12))
    row_out = row_attend(pattern, count, lines.reshape(-1, lines.shape[-1]))
    row_out = lax.all_to_all(row_out.reshape(row_span, col_span, -1), "cols", 0, 0, tiled=True)
    col_out = col_attend(me, col_pattern, col_count, pieces)
    col_out = swap_pieces(col_out)
    others = [by_xor(w, "rows", (1,))[0] for w in weights]
    half, heads = project_first(
        place,
        row_out,
        col_out,
        weights,
        out_weight.shape[1] * peers * lax.axis_size("cols"),
    )
    projected = project_second(place, heads, others, half)
    return projected.reshape(row_span, col_span, projected.shape[-1])


def solution(mesh):
    placed = (
        P("rows", "cols", None),
        P("rows", "cols", None),
        P("rows", "cols", None),
        P(None, ("rows", "cols")),
        P("rows", None, None),
        P("rows"),
        P("cols", None, None),
        P("cols"),
    )
    return jax.shard_map(
        body, mesh=mesh, in_specs=placed, out_specs=P("rows", "cols", None), check_vma=False
    )
```

```python
import functools
import math

import jax
import jax.numpy as jnp
from jax import lax
from jax.experimental import pallas as pl
from jax.experimental.pallas import tpu as pltpu
from jax.sharding import PartitionSpec as P


HR = 4
HC = 4
HD = 128
BLK = 32
NEG_FILL = -1e30
UNROLL = 4
EXP_SCALE = HD ** (-0.5) * math.log2(math.e)


def in_place(x):
    return pltpu.with_memory_space_constraint(x, pltpu.VMEM)


def row_pack_kernel(q_ref, k_ref, v_ref, out_ref):
    width = HR * HD
    out_ref[:, :, 0:width] = q_ref[...]
    out_ref[:, :, width : 2 * width] = k_ref[...]
    out_ref[:, :, 2 * width : 3 * width] = v_ref[...]


def row_pack(q, k, v):
    span, cells, _ = q.shape
    width = HR * HD
    step = 4
    part = pl.BlockSpec((step, cells, width), lambda i: (i, 0, 0))
    return pl.pallas_call(
        row_pack_kernel,
        grid=(span // step,),
        in_specs=[part, part, part],
        out_specs=pl.BlockSpec((step, cells, 3 * width), lambda i: (i, 0, 0)),
        out_shape=jax.ShapeDtypeStruct((span, cells, 3 * width), q.dtype),
        name="row_pack",
    )(q, k, v)


def col_pack_kernel(me_ref, q_ref, k_ref, v_ref, *rest):
    outs, (wide, buf, sem) = rest[:-3], rest[-3:]
    peers = len(outs)
    width = HC * HD
    span, own, _ = q_ref.shape
    step = pl.program_id(0)
    slot = lax.rem(step, 2)

    @pl.when(step >= 2)
    def _():
        pltpu.make_async_copy(buf.at[slot], outs[0], sem.at[slot]).wait()

    for t, ref in enumerate((q_ref, k_ref, v_ref)):
        for h in range(HC):
            lanes = slice(h * HD, (h + 1) * HD)
            wide[t * HC + h] = ref[:, :, lanes].reshape(span * own, HD).astype(jnp.float32)
    for t in range(3):
        for h in range(HC):
            for j in range(own):
                line = wide[t * HC + h, pl.ds(j, span, stride=own), :]
                at = t * width + h * HD
                buf[slot, j, :, at : at + HD] = line.astype(jnp.bfloat16)
    for s in range(peers):

        @pl.when(step == s)
        def _(s=s):
            pltpu.make_async_copy(buf.at[slot], outs[s], sem.at[slot]).start()

    @pl.when(step == peers - 1)
    def _():
        pltpu.make_async_copy(buf.at[1 - slot], outs[0], sem.at[1 - slot]).wait()
        pltpu.make_async_copy(buf.at[slot], outs[0], sem.at[slot]).wait()


def col_pack(me, q, k, v, peers):
    span, cells, _ = q.shape
    width = HC * HD
    own = cells // peers
    part = pl.BlockSpec((span, own, width), lambda s, me: (0, me[0] ^ s, 1))
    piece = (own, span, 3 * width)
    return pl.pallas_call(
        col_pack_kernel,
        grid_spec=pltpu.PrefetchScalarGridSpec(
            num_scalar_prefetch=1,
            grid=(peers,),
            in_specs=[part, part, part],
            out_specs=[pl.BlockSpec(memory_space=pl.ANY)] * peers,
            scratch_shapes=[
                pltpu.VMEM((3 * HC, span * own, HD), jnp.float32),
                pltpu.VMEM((2,) + piece, q.dtype),
                pltpu.SemaphoreType.DMA((2,)),
            ],
        ),
        out_shape=[jax.ShapeDtypeStruct(piece, q.dtype)] * peers,
        name="col_pack",
    )(me, q, k, v)


def row_attend_kernel(pattern_ref, count_ref, x_ref, out_ref, *, chosen):
    width = HR * HD
    count = count_ref[0]
    per = x_ref.shape[1] // BLK
    blocks = x_ref.shape[0] * per
    key_lane = lax.broadcasted_iota(jnp.int32, (1, chosen * BLK), 1)
    slot_of = key_lane // BLK
    in_block = key_lane - slot_of * BLK
    query_row = lax.broadcasted_iota(jnp.int32, (BLK, 1), 0)
    zero = jnp.zeros((BLK, HD), jnp.bfloat16)

    def block(b, lanes):
        at = pl.multiple_of(lax.rem(b, per) * BLK, BLK)
        return x_ref[lax.div(b, per), pl.ds(at, BLK), lanes]

    def stage_scores(n):
        q = block(n, slice(0, width))
        keys = []
        limit = jnp.zeros((1, chosen * BLK), jnp.int32)
        for s in range(chosen):
            b = pattern_ref[n * chosen + s]
            keys.append(block(b, slice(width, 2 * width)))
            limit = jnp.where(slot_of == s, count - b * BLK, limit)
        keys = jnp.concatenate(keys, axis=0)
        live = in_block < limit
        spread = jnp.concatenate(
            [
                jnp.concatenate(
                    [q[:, h * HD : (h + 1) * HD] if g == h else zero for g in range(HR)], axis=1
                )
                for h in range(HR)
            ],
            axis=0,
        )
        scores = lax.dot_general(
            spread, keys, (((1,), (1,)), ((), ())), preferred_element_type=jnp.float32
        )
        return jnp.where(live, scores, NEG_FILL)

    def stage_values(n, weights, total):
        at = pl.multiple_of(n * BLK, BLK)
        values = []
        for s in range(chosen):
            values.append(block(pattern_ref[n * chosen + s], slice(2 * width, 3 * width)))
        values = jnp.concatenate(values, axis=0)
        query_live = (query_row + n * BLK) < count
        for pair in range(HR // 2):
            rows = slice(pair * 2 * BLK, (pair + 1) * 2 * BLK)
            lanes = slice(pair * 2 * HD, (pair + 1) * 2 * HD)
            added = lax.dot_general(
                weights[rows],
                values[:, lanes],
                (((1,), (0,)), ((), ())),
                preferred_element_type=jnp.float32,
            )
            for g in range(2):
                h = pair * 2 + g
                part = added[g * BLK : (g + 1) * BLK, g * HD : (g + 1) * HD]
                safe = jnp.where(query_live, total[h * BLK : (h + 1) * BLK], 1.0)
                done = jnp.where(query_live, part / safe, 0.0)
                out_ref[pl.ds(at, BLK), h * HD : (h + 1) * HD] = done.astype(jnp.bfloat16)

    def group(g, _):
        blocks_here = [g * UNROLL + u for u in range(UNROLL)]
        scores = [stage_scores(n) for n in blocks_here]
        tops = [jnp.max(s, axis=1, keepdims=True) for s in scores]
        weights = [jnp.exp2((s - m) * EXP_SCALE) for s, m in zip(scores, tops)]
        totals = [jnp.sum(w, axis=1, keepdims=True) for w in weights]
        for n, w, t in zip(blocks_here, weights, totals):
            stage_values(n, w.astype(jnp.bfloat16), t)
        return 0

    lax.fori_loop(0, blocks // UNROLL, group, 0)


def row_attend(pattern, count, x):
    cells = x.shape[0] * x.shape[1]
    chosen = pattern.shape[-1]
    return pl.pallas_call(
        functools.partial(row_attend_kernel, chosen=chosen),
        grid_spec=pltpu.PrefetchScalarGridSpec(
            num_scalar_prefetch=2,
            grid=(1,),
            in_specs=[pl.BlockSpec(memory_space=pltpu.VMEM)],
            out_specs=pl.BlockSpec((cells, HR * HD), lambda i, *_: (0, 0)),
        ),
        out_shape=jax.ShapeDtypeStruct((cells, HR * HD), x.dtype),
        name="row_attend",
    )(pattern.reshape(-1), count, in_place(x))


def col_attend_kernel(me_ref, pattern_ref, count_ref, *rest, chosen, lines):
    peers = (len(rest) - 2) // 2
    pieces, outs, (line, held) = rest[:peers], rest[peers : 2 * peers], rest[2 * peers :]
    width = HC * HD
    me = me_ref[0]
    step = pl.program_id(0)
    span = pieces[0].shape[1]
    cells = peers * span
    own = held.shape[1] // cells
    blocks = cells // BLK
    key_at = lax.broadcasted_iota(jnp.int32, (1, cells), 1)
    key_block = key_at // BLK
    query_row = lax.broadcasted_iota(jnp.int32, (cells, 1), 0)
    for u in range(lines):
        for s in range(peers):
            line[u, pl.ds(pl.multiple_of((me ^ s) * span, span), span), :] = pieces[s][step * lines + u]
    jobs, scores = [], []
    for u in range(lines):
        j = step * lines + u
        first = me * own + j
        count = count_ref[first]
        rows = []
        for n in range(blocks):
            listed = key_block == pattern_ref[(first * blocks + n) * chosen]
            for s in range(1, chosen):
                listed = listed | (key_block == pattern_ref[(first * blocks + n) * chosen + s])
            row = jnp.where(listed & (key_at < count), 0.0, NEG_FILL)
            rows.append(jnp.broadcast_to(row, (BLK, cells)))
        bias = jnp.concatenate(rows, axis=0)
        query_live = query_row < count
        for h in range(HC):
            q = line[u, :, h * HD : (h + 1) * HD]
            k = line[u, :, width + h * HD : width + (h + 1) * HD]
            product = lax.dot_general(
                q, k, (((1,), (1,)), ((), ())), preferred_element_type=jnp.float32
            )
            scores.append(jnp.where(bias < 0.0, NEG_FILL, product))
            jobs.append((u, j, h, query_live))
    tops = [jnp.max(s, axis=1, keepdims=True) for s in scores]
    weights = [jnp.exp2((s - m) * EXP_SCALE) for s, m in zip(scores, tops)]
    totals = [jnp.sum(w, axis=1, keepdims=True) for w in weights]
    for (u, j, h, query_live), w, total in zip(jobs, weights, totals):
        v = line[u, :, 2 * width + h * HD : 2 * width + (h + 1) * HD]
        added = lax.dot_general(
            w.astype(jnp.bfloat16), v, (((1,), (0,)), ((), ())), preferred_element_type=jnp.float32
        )
        safe = jnp.where(query_live, total, 1.0)
        done = jnp.where(query_live, added / safe, 0.0)
        held[h, pl.ds(j, cells, stride=own), :] = done

    @pl.when(step == pl.num_programs(0) - 1)
    def _():
        for s in range(peers):
            at = pl.multiple_of((me ^ s) * span * own, span * own)
            for h in range(HC):
                part = held[h, pl.ds(at, span * own), :].reshape(span, own, HD)
                outs[s][:, :, h * HD : (h + 1) * HD] = part.astype(jnp.bfloat16)


def col_attend(me, pattern, count, pieces):
    peers = len(pieces)
    own, span, wide = pieces[0].shape
    width = HC * HD
    chosen = pattern.shape[-1]
    lines = 2
    result = (span, own, width)
    return pl.pallas_call(
        functools.partial(col_attend_kernel, chosen=chosen, lines=lines),
        grid_spec=pltpu.PrefetchScalarGridSpec(
            num_scalar_prefetch=3,
            grid=(own // lines,),
            in_specs=[pl.BlockSpec(memory_space=pltpu.VMEM)] * peers,
            out_specs=[pl.BlockSpec(result, lambda j, *_: (0, 0, 0))] * peers,
            scratch_shapes=[
                pltpu.VMEM((lines, peers * span, wide), jnp.bfloat16),
                pltpu.VMEM((HC, own * peers * span, HD), jnp.float32),
            ],
        ),
        out_shape=[jax.ShapeDtypeStruct(result, jnp.bfloat16)] * peers,
        name="col_attend",
    )(me, pattern.reshape(-1), count, *[in_place(p) for p in pieces])


def weight_copies(place, weights, line, sem, turn, slot):
    _, near, span, _ = weights[0].shape
    plane = place[1]
    copies = []
    for sx, weight in enumerate(weights):
        for sz in range(near):
            at = ((plane // near ^ sx) * near + (lax.rem(plane, near) ^ sz)) * span
            target = line.at[slot, pl.ds(pl.multiple_of(at, span), span), :]
            copies.append(pltpu.make_async_copy(weight.at[turn, sz], target, sem.at[slot]))
    return copies


def project_block(place, heads, weights, line, sem, out_ref):
    turn = pl.program_id(0)
    slot = lax.rem(turn, 2)

    @pl.when(turn + 1 < pl.num_programs(0))
    def _():
        for copy in weight_copies(place, weights, line, sem, turn + 1, 1 - slot):
            copy.start()

    for copy in weight_copies(place, weights, line, sem, turn, slot):
        copy.wait()
    out_ref[...] = lax.dot_general(
        heads[...].reshape(-1, heads.shape[2]),
        line[slot],
        (((1,), (1,)), ((), ())),
        preferred_element_type=jnp.float32,
    ).astype(jnp.bfloat16)


def project_first_kernel(place, row_ref, *rest, quarter):
    pieces, weights = rest[: -4 - quarter], rest[-4 - quarter : -4]
    out_ref, heads, line, sem = rest[-4:]
    width = HR * HD
    own = pieces[0].shape[1]

    @pl.when(pl.program_id(0) == 0)
    def _():
        for copy in weight_copies(place, weights, line, sem, 0, 0):
            copy.start()
        me = place[0]
        odd = lax.rem(me, 2) == 1
        heads[:, :, 0:width] = row_ref[...]
        for s in range(0, len(pieces), 2):
            a = pieces[s][...].astype(jnp.float32)
            b = pieces[s + 1][...].astype(jnp.float32)
            both = jnp.concatenate([jnp.where(odd, b, a), jnp.where(odd, a, b)], axis=1)
            at = pl.multiple_of(((me ^ s) // 2) * 2 * own, 2 * own)
            heads[:, pl.ds(at, 2 * own), width:] = both.astype(jnp.bfloat16)

    project_block(place, heads, weights, line, sem, out_ref)


def project_second_kernel(place, heads, *rest, quarter):
    weights, (_, out_ref, line, sem) = rest[:quarter], rest[quarter:]

    @pl.when(pl.program_id(0) == 0)
    def _():
        for copy in weight_copies(place, weights, line, sem, 0, 0):
            copy.start()

    project_block(place, heads, weights, line, sem, out_ref)


def whole(a):
    return pl.BlockSpec(a.shape, lambda j, *_: (0,) * a.ndim)


def project_first(place, row_out, pieces, weights, outs):
    span, cells, _ = row_out.shape
    turns, near, part, channels = weights[0].shape
    tile = len(weights) * near * part
    return pl.pallas_call(
        functools.partial(project_first_kernel, quarter=len(weights)),
        grid_spec=pltpu.PrefetchScalarGridSpec(
            num_scalar_prefetch=1,
            grid=(turns,),
            in_specs=[pl.BlockSpec(memory_space=pltpu.VMEM)] * (1 + len(pieces))
            + [pl.BlockSpec(memory_space=pl.ANY)] * len(weights),
            out_specs=[
                pl.BlockSpec((span * cells, tile), lambda j, at: (0, at[0] ^ (2 * j))),
                pl.BlockSpec((span, cells, channels), lambda j, *_: (0, 0, 0)),
            ],
            scratch_shapes=[
                pltpu.VMEM((2, tile, channels), jnp.bfloat16),
                pltpu.SemaphoreType.DMA((2,)),
            ],
        ),
        out_shape=[
            jax.ShapeDtypeStruct((span * cells, outs), jnp.bfloat16),
            jax.ShapeDtypeStruct((span, cells, channels), jnp.bfloat16),
        ],
        name="project_first",
    )(place, in_place(row_out), *[in_place(p) for p in pieces], *weights)


def project_second(place, heads, weights, kept):
    span, cells, channels = heads.shape
    turns, near, part, _ = weights[0].shape
    tile = len(weights) * near * part
    return pl.pallas_call(
        functools.partial(project_second_kernel, quarter=len(weights)),
        grid_spec=pltpu.PrefetchScalarGridSpec(
            num_scalar_prefetch=1,
            grid=(turns,),
            in_specs=[whole(heads)] + [pl.BlockSpec(memory_space=pl.ANY)] * (1 + len(weights)),
            out_specs=pl.BlockSpec((span * cells, tile), lambda j, at: (0, at[0] ^ (2 * j + 1))),
            scratch_shapes=[
                pltpu.VMEM((2, tile, channels), jnp.bfloat16),
                pltpu.SemaphoreType.DMA((2,)),
            ],
        ),
        out_shape=jax.ShapeDtypeStruct(kept.shape, jnp.bfloat16),
        input_output_aliases={2 + len(weights): 0},
        name="project_second",
    )(place, heads, *weights, kept)


def by_xor(x, axis, masks):
    size = lax.axis_size(axis)
    return [lax.ppermute(x, axis, [(d, d ^ s) for d in range(size)]) for s in masks]


def swap_pieces(pieces):
    peers = len(pieces)
    return [pieces[0]] + [
        lax.ppermute(pieces[s], "rows", [(d, d ^ s) for d in range(peers)])
        for s in range(1, peers)
    ]


def body(
    query_cells, key_cells, value_cells, out_weight, row_pattern, row_count, col_pattern, col_count
):
    row_span, col_span, _ = query_cells.shape
    peers = lax.axis_size("rows")
    row_share = row_span // lax.axis_size("cols")
    me = lax.axis_index("rows").astype(jnp.int32).reshape(1)
    row_first = lax.axis_index("cols") * row_share
    pattern = lax.dynamic_slice_in_dim(row_pattern, row_first, row_share, 0)
    count = lax.dynamic_slice_in_dim(row_count, row_first, row_share, 0)

    place = jnp.stack([lax.axis_index("rows"), lax.axis_index("cols")]).astype(jnp.int32)

    shard = out_weight.T
    along_z = [shard] + by_xor(shard, "cols", (1, 2, 3))
    packed = row_pack(query_cells, key_cells, value_cells)
    lines = lax.all_to_all(packed, "cols", 0, 0, tiled=True)
    held = jnp.stack(along_z)
    along_y = [held] + by_xor(held, "rows", (2, 4, 6))
    sent = col_pack(me, query_cells, key_cells, value_cells, peers)
    pieces = swap_pieces(sent)
    held = jnp.stack(along_y)
    weights = [held] + by_xor(held, "cols", (4, 8, 12))
    row_out = row_attend(pattern, count, lines)
    row_out = lax.all_to_all(row_out.reshape(row_span, col_span, -1), "cols", 0, 0, tiled=True)
    col_out = col_attend(me, col_pattern, col_count, pieces)
    col_out = swap_pieces(col_out)
    others = [by_xor(w, "rows", (1,))[0] for w in weights]
    half, heads = project_first(
        place,
        row_out,
        col_out,
        weights,
        out_weight.shape[1] * peers * lax.axis_size("cols"),
    )
    projected = project_second(place, heads, others, half)
    return projected.reshape(row_span, col_span, projected.shape[-1])


def solution(mesh):
    placed = (
        P("rows", "cols", None),
        P("rows", "cols", None),
        P("rows", "cols", None),
        P(None, ("rows", "cols")),
        P("rows", None, None),
        P("rows"),
        P("cols", None, None),
        P("cols"),
    )
    return jax.shard_map(
        body, mesh=mesh, in_specs=placed, out_specs=P("rows", "cols", None), check_vma=False
    )
```

```python
import functools
import math

import jax
import jax.numpy as jnp
from jax import lax
from jax.experimental import pallas as pl
from jax.experimental.pallas import tpu as pltpu
from jax.sharding import PartitionSpec as P


HR = 4
HC = 4
HD = 128
BLK = 32
NEG_FILL = -1e30
UNROLL = 4
EXP_SCALE = HD ** (-0.5) * math.log2(math.e)


def in_place(x):
    return pltpu.with_memory_space_constraint(x, pltpu.VMEM)


def row_pack_kernel(q_ref, k_ref, v_ref, out_ref):
    width = HR * HD
    out_ref[:, :, 0:width] = q_ref[...]
    out_ref[:, :, width : 2 * width] = k_ref[...]
    out_ref[:, :, 2 * width : 3 * width] = v_ref[...]


def row_pack(q, k, v):
    span, cells, _ = q.shape
    width = HR * HD
    step = 4
    part = pl.BlockSpec((step, cells, width), lambda i: (i, 0, 0))
    return pl.pallas_call(
        row_pack_kernel,
        grid=(span // step,),
        in_specs=[part, part, part],
        out_specs=pl.BlockSpec((step, cells, 3 * width), lambda i: (i, 0, 0)),
        out_shape=jax.ShapeDtypeStruct((span, cells, 3 * width), q.dtype),
        name="row_pack",
    )(q, k, v)


def col_pack_kernel(me_ref, q_ref, k_ref, v_ref, *rest):
    outs, (wide, buf, sem) = rest[:-3], rest[-3:]
    peers = len(outs)
    width = HC * HD
    span, own, _ = q_ref.shape
    step = pl.program_id(0)
    slot = lax.rem(step, 2)

    @pl.when(step >= 2)
    def _():
        pltpu.make_async_copy(buf.at[slot], outs[0], sem.at[slot]).wait()

    for t, ref in enumerate((q_ref, k_ref, v_ref)):
        for h in range(HC):
            lanes = slice(h * HD, (h + 1) * HD)
            wide[t * HC + h] = ref[:, :, lanes].reshape(span * own, HD).astype(jnp.float32)
    for t in range(3):
        for h in range(HC):
            for j in range(own):
                line = wide[t * HC + h, pl.ds(j, span, stride=own), :]
                at = t * width + h * HD
                buf[slot, j, :, at : at + HD] = line.astype(jnp.bfloat16)
    for s in range(peers):

        @pl.when(step == s)
        def _(s=s):
            pltpu.make_async_copy(buf.at[slot], outs[s], sem.at[slot]).start()

    @pl.when(step == peers - 1)
    def _():
        pltpu.make_async_copy(buf.at[1 - slot], outs[0], sem.at[1 - slot]).wait()
        pltpu.make_async_copy(buf.at[slot], outs[0], sem.at[slot]).wait()


def col_pack(me, q, k, v, peers):
    span, cells, _ = q.shape
    width = HC * HD
    own = cells // peers
    part = pl.BlockSpec((span, own, width), lambda s, me: (0, me[0] ^ s, 1))
    piece = (own, span, 3 * width)
    return pl.pallas_call(
        col_pack_kernel,
        grid_spec=pltpu.PrefetchScalarGridSpec(
            num_scalar_prefetch=1,
            grid=(peers,),
            in_specs=[part, part, part],
            out_specs=[pl.BlockSpec(memory_space=pl.ANY)] * peers,
            scratch_shapes=[
                pltpu.VMEM((3 * HC, span * own, HD), jnp.float32),
                pltpu.VMEM((2,) + piece, q.dtype),
                pltpu.SemaphoreType.DMA((2,)),
            ],
        ),
        out_shape=[jax.ShapeDtypeStruct(piece, q.dtype)] * peers,
        name="col_pack",
    )(me, q, k, v)


def row_attend_kernel(pattern_ref, count_ref, x_ref, out_ref, *, chosen):
    width = HR * HD
    count = count_ref[0]
    per = x_ref.shape[1] // BLK
    blocks = x_ref.shape[0] * per
    key_lane = lax.broadcasted_iota(jnp.int32, (1, chosen * BLK), 1)
    slot_of = key_lane // BLK
    in_block = key_lane - slot_of * BLK
    query_row = lax.broadcasted_iota(jnp.int32, (BLK, 1), 0)
    zero = jnp.zeros((BLK, HD), jnp.bfloat16)

    def block(b, lanes):
        at = pl.multiple_of(lax.rem(b, per) * BLK, BLK)
        return x_ref[lax.div(b, per), pl.ds(at, BLK), lanes]

    def stage_scores(n):
        q = block(n, slice(0, width))
        keys = []
        limit = jnp.zeros((1, chosen * BLK), jnp.int32)
        for s in range(chosen):
            b = pattern_ref[n * chosen + s]
            keys.append(block(b, slice(width, 2 * width)))
            limit = jnp.where(slot_of == s, count - b * BLK, limit)
        keys = jnp.concatenate(keys, axis=0)
        live = in_block < limit
        spread = jnp.concatenate(
            [
                jnp.concatenate(
                    [q[:, h * HD : (h + 1) * HD] if g == h else zero for g in range(HR)], axis=1
                )
                for h in range(HR)
            ],
            axis=0,
        )
        scores = lax.dot_general(
            spread, keys, (((1,), (1,)), ((), ())), preferred_element_type=jnp.float32
        )
        return jnp.where(live, scores, NEG_FILL)

    def stage_values(n, weights, total):
        at = pl.multiple_of(n * BLK, BLK)
        values = []
        for s in range(chosen):
            values.append(block(pattern_ref[n * chosen + s], slice(2 * width, 3 * width)))
        values = jnp.concatenate(values, axis=0)
        query_live = (query_row + n * BLK) < count
        for pair in range(HR // 2):
            rows = slice(pair * 2 * BLK, (pair + 1) * 2 * BLK)
            lanes = slice(pair * 2 * HD, (pair + 1) * 2 * HD)
            added = lax.dot_general(
                weights[rows],
                values[:, lanes],
                (((1,), (0,)), ((), ())),
                preferred_element_type=jnp.float32,
            )
            for g in range(2):
                h = pair * 2 + g
                part = added[g * BLK : (g + 1) * BLK, g * HD : (g + 1) * HD]
                safe = jnp.where(query_live, total[h * BLK : (h + 1) * BLK], 1.0)
                done = jnp.where(query_live, part / safe, 0.0)
                out_ref[pl.ds(at, BLK), h * HD : (h + 1) * HD] = done.astype(jnp.bfloat16)

    def group(g, _):
        blocks_here = [g * UNROLL + u for u in range(UNROLL)]
        scores = [stage_scores(n) for n in blocks_here]
        tops = [jnp.max(s, axis=1, keepdims=True) for s in scores]
        weights = [jnp.exp2((s - m) * EXP_SCALE) for s, m in zip(scores, tops)]
        totals = [jnp.sum(w, axis=1, keepdims=True) for w in weights]
        for n, w, t in zip(blocks_here, weights, totals):
            stage_values(n, w.astype(jnp.bfloat16), t)
        return 0

    lax.fori_loop(0, blocks // UNROLL, group, 0)


def row_attend(pattern, count, x):
    cells = x.shape[0] * x.shape[1]
    chosen = pattern.shape[-1]
    return pl.pallas_call(
        functools.partial(row_attend_kernel, chosen=chosen),
        grid_spec=pltpu.PrefetchScalarGridSpec(
            num_scalar_prefetch=2,
            grid=(1,),
            in_specs=[pl.BlockSpec(memory_space=pltpu.VMEM)],
            out_specs=pl.BlockSpec((cells, HR * HD), lambda i, *_: (0, 0)),
        ),
        out_shape=jax.ShapeDtypeStruct((cells, HR * HD), x.dtype),
        name="row_attend",
    )(pattern.reshape(-1), count, in_place(x))


def col_attend_kernel(me_ref, pattern_ref, count_ref, *rest, chosen, lines):
    peers = (len(rest) - 2) // 2
    pieces, outs, (line, held) = rest[:peers], rest[peers : 2 * peers], rest[2 * peers :]
    width = HC * HD
    me = me_ref[0]
    step = pl.program_id(0)
    span = pieces[0].shape[1]
    cells = peers * span
    own = held.shape[1] // cells
    blocks = cells // BLK
    key_at = lax.broadcasted_iota(jnp.int32, (1, cells), 1)
    key_block = key_at // BLK
    query_row = lax.broadcasted_iota(jnp.int32, (cells, 1), 0)
    for u in range(lines):
        for s in range(peers):
            line[u, pl.ds(pl.multiple_of((me ^ s) * span, span), span), :] = pieces[s][step * lines + u]
    jobs, scores = [], []
    for u in range(lines):
        j = step * lines + u
        first = me * own + j
        count = count_ref[first]
        rows = []
        for n in range(blocks):
            listed = key_block == pattern_ref[(first * blocks + n) * chosen]
            for s in range(1, chosen):
                listed = listed | (key_block == pattern_ref[(first * blocks + n) * chosen + s])
            row = jnp.where(listed & (key_at < count), 0.0, NEG_FILL)
            rows.append(jnp.broadcast_to(row, (BLK, cells)))
        bias = jnp.concatenate(rows, axis=0)
        query_live = query_row < count
        for h in range(HC):
            q = line[u, :, h * HD : (h + 1) * HD]
            k = line[u, :, width + h * HD : width + (h + 1) * HD]
            product = lax.dot_general(
                q, k, (((1,), (1,)), ((), ())), preferred_element_type=jnp.float32
            )
            scores.append(jnp.where(bias < 0.0, NEG_FILL, product))
            jobs.append((u, j, h, query_live))
    tops = [jnp.max(s, axis=1, keepdims=True) for s in scores]
    weights = [jnp.exp2((s - m) * EXP_SCALE) for s, m in zip(scores, tops)]
    totals = [jnp.sum(w, axis=1, keepdims=True) for w in weights]
    for (u, j, h, query_live), w, total in zip(jobs, weights, totals):
        v = line[u, :, 2 * width + h * HD : 2 * width + (h + 1) * HD]
        added = lax.dot_general(
            w.astype(jnp.bfloat16), v, (((1,), (0,)), ((), ())), preferred_element_type=jnp.float32
        )
        safe = jnp.where(query_live, total, 1.0)
        done = jnp.where(query_live, added / safe, 0.0)
        held[h, pl.ds(j, cells, stride=own), :] = done

    @pl.when(step == pl.num_programs(0) - 1)
    def _():
        for s in range(peers):
            at = pl.multiple_of((me ^ s) * span * own, span * own)
            for h in range(HC):
                part = held[h, pl.ds(at, span * own), :].reshape(span, own, HD)
                outs[s][:, :, h * HD : (h + 1) * HD] = part.astype(jnp.bfloat16)


def col_attend(me, pattern, count, pieces):
    peers = len(pieces)
    own, span, wide = pieces[0].shape
    width = HC * HD
    chosen = pattern.shape[-1]
    lines = 2
    result = (span, own, width)
    return pl.pallas_call(
        functools.partial(col_attend_kernel, chosen=chosen, lines=lines),
        grid_spec=pltpu.PrefetchScalarGridSpec(
            num_scalar_prefetch=3,
            grid=(own // lines,),
            in_specs=[pl.BlockSpec(memory_space=pltpu.VMEM)] * peers,
            out_specs=[pl.BlockSpec(result, lambda j, *_: (0, 0, 0))] * peers,
            scratch_shapes=[
                pltpu.VMEM((lines, peers * span, wide), jnp.bfloat16),
                pltpu.VMEM((HC, own * peers * span, HD), jnp.float32),
            ],
        ),
        out_shape=[jax.ShapeDtypeStruct(result, jnp.bfloat16)] * peers,
        name="col_attend",
    )(me, pattern.reshape(-1), count, pieces[0], *[in_place(p) for p in pieces[1:]])


def project_kernel(place, row_ref, *rest, peers, near):
    pieces, (out_ref, heads, line, sem) = rest[:peers], rest[-4:]
    weights = rest[peers:-4]
    width = HR * HD
    own = pieces[0].shape[1]
    me, plane = place[0], place[1]
    step = pl.program_id(0)
    slot = lax.rem(step, 2)
    at_x, at_z = lax.div(plane, near), lax.rem(plane, near)

    def fetch(step, slot):
        turn = lax.rem(step, near)
        for core in range(2):

            @pl.when(lax.div(step, near) == core)
            def _(core=core):
                group = weights[2 * near * core : 2 * near * (core + 1)]
                for a in range(near):
                    for b in range(near):
                        for half, (x, z) in enumerate(((a, b), (b, a))):
                            source = group[half * near + a].at[turn, b]
                            span, wide = source.shape
                            at = ((at_x ^ x) * near + (at_z ^ z)) * span
                            target = line.at[
                                slot,
                                pl.ds(pl.multiple_of(at, span), span),
                                pl.ds(half * wide, wide),
                            ]
                            pltpu.make_async_copy(source, target, sem.at[slot]).start()

    @pl.when(step == 0)
    def _():
        fetch(step, slot)
        odd = lax.rem(me, 2) == 1
        heads[:, :, 0:width] = row_ref[...]
        for s in range(0, peers, 2):
            a = pieces[s][...].astype(jnp.float32)
            b = pieces[s + 1][...].astype(jnp.float32)
            both = jnp.concatenate([jnp.where(odd, b, a), jnp.where(odd, a, b)], axis=1)
            at = pl.multiple_of(((me ^ s) // 2) * 2 * own, 2 * own)
            heads[:, pl.ds(at, 2 * own), width:] = both.astype(jnp.bfloat16)

    @pl.when(step + 1 < pl.num_programs(0))
    def _():
        fetch(step + 1, 1 - slot)

    pltpu.make_async_copy(line.at[slot], line.at[slot], sem.at[slot]).wait()
    out_ref[...] = lax.dot_general(
        heads[...].reshape(-1, heads.shape[2]),
        line[slot],
        (((1,), (1,)), ((), ())),
        preferred_element_type=jnp.float32,
    ).astype(jnp.bfloat16)


def project(place, row_out, pieces, weights, outs):
    span, cells, _ = row_out.shape
    turns, near, part, wide = weights[0].shape
    channels = 2 * wide
    tile = near * near * part
    held = pl.BlockSpec(memory_space=pltpu.VMEM)

    def target(j, at):
        return 0, at[0] ^ (2 * lax.rem(j, turns) + lax.div(j, turns))

    return pl.pallas_call(
        functools.partial(project_kernel, peers=len(pieces), near=near),
        grid_spec=pltpu.PrefetchScalarGridSpec(
            num_scalar_prefetch=1,
            grid=(2 * turns,),
            in_specs=[held] * (1 + len(pieces))
            + [pl.BlockSpec(memory_space=pl.ANY)] * len(weights),
            out_specs=pl.BlockSpec((span * cells, tile), target),
            scratch_shapes=[
                pltpu.VMEM((span, cells, channels), jnp.bfloat16),
                pltpu.VMEM((2, tile, channels), jnp.bfloat16),
                pltpu.SemaphoreType.DMA((2,)),
            ],
        ),
        out_shape=jax.ShapeDtypeStruct((span * cells, outs), jnp.bfloat16),
        name="project",
    )(place, in_place(row_out), pieces[0], *[in_place(p) for p in pieces[1:]], *weights)


def by_xor(x, axis, masks):
    size = lax.axis_size(axis)
    return [lax.ppermute(x, axis, [(d, d ^ s) for d in range(size)]) for s in masks]


def swap_pieces(pieces):
    peers = len(pieces)
    return [pieces[0]] + [
        lax.ppermute(pieces[s], "rows", [(d, d ^ s) for d in range(peers)])
        for s in range(1, peers)
    ]


def join_kernel(*refs):
    for i, ref in enumerate(refs[:-1]):
        refs[-1][i] = ref[...]


def join(parts):
    return pl.pallas_call(
        join_kernel,
        in_specs=[pl.BlockSpec(memory_space=pltpu.VMEM)] * len(parts),
        out_specs=pl.BlockSpec(memory_space=pltpu.VMEM),
        out_shape=jax.ShapeDtypeStruct((len(parts),) + parts[0].shape, parts[0].dtype),
        name="join",
    )(*[in_place(p) for p in parts])


def body(
    query_cells, key_cells, value_cells, out_weight, row_pattern, row_count, col_pattern, col_count
):
    row_span, col_span, _ = query_cells.shape
    peers = lax.axis_size("rows")
    row_share = row_span // lax.axis_size("cols")
    me = lax.axis_index("rows").astype(jnp.int32).reshape(1)
    row_first = lax.axis_index("cols") * row_share
    pattern = lax.dynamic_slice_in_dim(row_pattern, row_first, row_share, 0)
    count = lax.dynamic_slice_in_dim(row_count, row_first, row_share, 0)

    place = jnp.stack([lax.axis_index("rows"), lax.axis_index("cols")]).astype(jnp.int32)

    shard = out_weight.T
    middle = shard.shape[1] // 2
    upper, lower = shard[:, :middle], shard[:, middle:]
    along_z = [upper] + by_xor(upper, "cols", (1, 2, 3))
    along_x = [lower] + by_xor(lower, "cols", (4, 8, 12))
    packed = row_pack(query_cells, key_cells, value_cells)
    lines = lax.all_to_all(packed, "cols", 0, 0, tiled=True)
    held = join(along_z + along_x)
    along_y = [held] + by_xor(held, "rows", (2, 4, 6))
    sent = col_pack(me, query_cells, key_cells, value_cells, peers)
    pieces = swap_pieces(sent)
    near = len(along_z)
    upper = jnp.stack([h[:near] for h in along_y])
    lower = jnp.stack([h[near:] for h in along_y])
    weights = [upper] + by_xor(upper, "cols", (4, 8, 12))
    weights += [lower] + by_xor(lower, "cols", (1, 2, 3))
    row_out = row_attend(pattern, count, lines)
    row_out = lax.all_to_all(row_out.reshape(row_span, col_span, -1), "cols", 0, 0, tiled=True)
    col_out = col_attend(me, col_pattern, col_count, pieces)
    col_out = swap_pieces(col_out)
    weights += [by_xor(w, "rows", (1,))[0] for w in weights]
    outs = out_weight.shape[1] * peers * lax.axis_size("cols")
    projected = project(place, row_out, col_out, weights, outs)
    return projected.reshape(row_span, col_span, projected.shape[-1])


def solution(mesh):
    placed = (
        P("rows", "cols", None),
        P("rows", "cols", None),
        P("rows", "cols", None),
        P(None, ("rows", "cols")),
        P("rows", None, None),
        P("rows"),
        P("cols", None, None),
        P("cols"),
    )
    return jax.shard_map(
        body, mesh=mesh, in_specs=placed, out_specs=P("rows", "cols", None), check_vma=False
    )
```

```python
import functools
import math

import jax
import jax.numpy as jnp
from jax import lax
from jax.experimental import pallas as pl
from jax.experimental.pallas import tpu as pltpu
from jax.sharding import PartitionSpec as P


HR = 4
HC = 4
HD = 128
BLK = 32
NEG_FILL = -1e30
UNROLL = 4
EXP_SCALE = HD ** (-0.5) * math.log2(math.e)


def grant(mebibytes):
    return pltpu.CompilerParams(vmem_limit_bytes=mebibytes << 20)


def in_place(x):
    return pltpu.with_memory_space_constraint(x, pltpu.VMEM)


def row_pack_kernel(q_ref, k_ref, v_ref, out_ref):
    width = HR * HD
    out_ref[:, :, 0:width] = q_ref[...]
    out_ref[:, :, width : 2 * width] = k_ref[...]
    out_ref[:, :, 2 * width : 3 * width] = v_ref[...]


def row_pack(q, k, v):
    span, cells, _ = q.shape
    width = HR * HD
    step = 4
    part = pl.BlockSpec((step, cells, width), lambda i: (i, 0, 0))
    return pl.pallas_call(
        row_pack_kernel,
        grid=(span // step,),
        in_specs=[part, part, part],
        out_specs=pl.BlockSpec((step, cells, 3 * width), lambda i: (i, 0, 0)),
        out_shape=jax.ShapeDtypeStruct((span, cells, 3 * width), q.dtype),
        compiler_params=grant(56),
        name="row_pack",
    )(q, k, v)


def col_pack_kernel(me_ref, q_ref, k_ref, v_ref, *rest):
    outs, (wide, buf, sem) = rest[:-3], rest[-3:]
    peers = len(outs)
    width = HC * HD
    span, own, _ = q_ref.shape
    step = pl.program_id(0)
    slot = lax.rem(step, 2)

    @pl.when(step >= 2)
    def _():
        pltpu.make_async_copy(buf.at[slot], outs[0], sem.at[slot]).wait()

    for t, ref in enumerate((q_ref, k_ref, v_ref)):
        for h in range(HC):
            lanes = slice(h * HD, (h + 1) * HD)
            wide[t * HC + h] = ref[:, :, lanes].reshape(span * own, HD).astype(jnp.float32)
    for t in range(3):
        for h in range(HC):
            for j in range(own):
                line = wide[t * HC + h, pl.ds(j, span, stride=own), :]
                at = t * width + h * HD
                buf[slot, j, :, at : at + HD] = line.astype(jnp.bfloat16)
    for s in range(peers):

        @pl.when(step == s)
        def _(s=s):
            pltpu.make_async_copy(buf.at[slot], outs[s], sem.at[slot]).start()

    @pl.when(step == peers - 1)
    def _():
        pltpu.make_async_copy(buf.at[1 - slot], outs[0], sem.at[1 - slot]).wait()
        pltpu.make_async_copy(buf.at[slot], outs[0], sem.at[slot]).wait()


def col_pack(me, q, k, v, peers):
    span, cells, _ = q.shape
    width = HC * HD
    own = cells // peers
    part = pl.BlockSpec((span, own, width), lambda s, me: (0, me[0] ^ s, 1))
    piece = (own, span, 3 * width)
    return pl.pallas_call(
        col_pack_kernel,
        grid_spec=pltpu.PrefetchScalarGridSpec(
            num_scalar_prefetch=1,
            grid=(peers,),
            in_specs=[part, part, part],
            out_specs=[pl.BlockSpec(memory_space=pl.ANY)] * peers,
            scratch_shapes=[
                pltpu.VMEM((3 * HC, span * own, HD), jnp.float32),
                pltpu.VMEM((2,) + piece, q.dtype),
                pltpu.SemaphoreType.DMA((2,)),
            ],
        ),
        out_shape=[jax.ShapeDtypeStruct(piece, q.dtype)] * peers,
        compiler_params=grant(56),
        name="col_pack",
    )(me, q, k, v)


def row_attend_kernel(pattern_ref, count_ref, x_ref, out_ref, *, chosen):
    width = HR * HD
    count = count_ref[0]
    per = x_ref.shape[1] // BLK
    blocks = x_ref.shape[0] * per
    key_lane = lax.broadcasted_iota(jnp.int32, (1, chosen * BLK), 1)
    slot_of = key_lane // BLK
    in_block = key_lane - slot_of * BLK
    query_row = lax.broadcasted_iota(jnp.int32, (BLK, 1), 0)
    zero = jnp.zeros((BLK, HD), jnp.bfloat16)

    def block(b, lanes):
        at = pl.multiple_of(lax.rem(b, per) * BLK, BLK)
        return x_ref[lax.div(b, per), pl.ds(at, BLK), lanes]

    def stage_scores(n):
        q = block(n, slice(0, width))
        keys = []
        limit = jnp.zeros((1, chosen * BLK), jnp.int32)
        for s in range(chosen):
            b = pattern_ref[n * chosen + s]
            keys.append(block(b, slice(width, 2 * width)))
            limit = jnp.where(slot_of == s, count - b * BLK, limit)
        keys = jnp.concatenate(keys, axis=0)
        live = in_block < limit
        spread = jnp.concatenate(
            [
                jnp.concatenate(
                    [q[:, h * HD : (h + 1) * HD] if g == h else zero for g in range(HR)], axis=1
                )
                for h in range(HR)
            ],
            axis=0,
        )
        scores = lax.dot_general(
            spread, keys, (((1,), (1,)), ((), ())), preferred_element_type=jnp.float32
        )
        return jnp.where(live, scores, NEG_FILL)

    def stage_values(n, weights, total):
        at = pl.multiple_of(n * BLK, BLK)
        values = []
        for s in range(chosen):
            values.append(block(pattern_ref[n * chosen + s], slice(2 * width, 3 * width)))
        values = jnp.concatenate(values, axis=0)
        query_live = (query_row + n * BLK) < count
        for pair in range(HR // 2):
            rows = slice(pair * 2 * BLK, (pair + 1) * 2 * BLK)
            lanes = slice(pair * 2 * HD, (pair + 1) * 2 * HD)
            added = lax.dot_general(
                weights[rows],
                values[:, lanes],
                (((1,), (0,)), ((), ())),
                preferred_element_type=jnp.float32,
            )
            for g in range(2):
                h = pair * 2 + g
                part = added[g * BLK : (g + 1) * BLK, g * HD : (g + 1) * HD]
                safe = jnp.where(query_live, total[h * BLK : (h + 1) * BLK], 1.0)
                done = jnp.where(query_live, part / safe, 0.0)
                out_ref[pl.ds(at, BLK), h * HD : (h + 1) * HD] = done.astype(jnp.bfloat16)

    def group(g, _):
        blocks_here = [g * UNROLL + u for u in range(UNROLL)]
        scores = [stage_scores(n) for n in blocks_here]
        tops = [jnp.max(s, axis=1, keepdims=True) for s in scores]
        weights = [jnp.exp2((s - m) * EXP_SCALE) for s, m in zip(scores, tops)]
        totals = [jnp.sum(w, axis=1, keepdims=True) for w in weights]
        for n, w, t in zip(blocks_here, weights, totals):
            stage_values(n, w.astype(jnp.bfloat16), t)
        return 0

    lax.fori_loop(0, blocks // UNROLL, group, 0)


def row_attend(pattern, count, x):
    cells = x.shape[0] * x.shape[1]
    chosen = pattern.shape[-1]
    return pl.pallas_call(
        functools.partial(row_attend_kernel, chosen=chosen),
        grid_spec=pltpu.PrefetchScalarGridSpec(
            num_scalar_prefetch=2,
            grid=(1,),
            in_specs=[pl.BlockSpec(memory_space=pltpu.VMEM)],
            out_specs=pl.BlockSpec((cells, HR * HD), lambda i, *_: (0, 0)),
        ),
        out_shape=jax.ShapeDtypeStruct((cells, HR * HD), x.dtype),
        compiler_params=grant(56),
        name="row_attend",
    )(pattern.reshape(-1), count, in_place(x))


def col_attend_kernel(me_ref, pattern_ref, count_ref, *rest, chosen, lines):
    peers = (len(rest) - 2) // 2
    pieces, outs, (line, held) = rest[:peers], rest[peers : 2 * peers], rest[2 * peers :]
    width = HC * HD
    me = me_ref[0]
    step = pl.program_id(0)
    span = pieces[0].shape[1]
    cells = peers * span
    own = held.shape[1] // cells
    blocks = cells // BLK
    key_at = lax.broadcasted_iota(jnp.int32, (1, cells), 1)
    key_block = key_at // BLK
    query_row = lax.broadcasted_iota(jnp.int32, (cells, 1), 0)
    for u in range(lines):
        for s in range(peers):
            line[u, pl.ds(pl.multiple_of((me ^ s) * span, span), span), :] = pieces[s][step * lines + u]
    jobs, scores = [], []
    for u in range(lines):
        j = step * lines + u
        first = me * own + j
        count = count_ref[first]
        rows = []
        for n in range(blocks):
            listed = key_block == pattern_ref[(first * blocks + n) * chosen]
            for s in range(1, chosen):
                listed = listed | (key_block == pattern_ref[(first * blocks + n) * chosen + s])
            row = jnp.where(listed & (key_at < count), 0.0, NEG_FILL)
            rows.append(jnp.broadcast_to(row, (BLK, cells)))
        bias = jnp.concatenate(rows, axis=0)
        query_live = query_row < count
        for h in range(HC):
            q = line[u, :, h * HD : (h + 1) * HD]
            k = line[u, :, width + h * HD : width + (h + 1) * HD]
            product = lax.dot_general(
                q, k, (((1,), (1,)), ((), ())), preferred_element_type=jnp.float32
            )
            scores.append(jnp.where(bias < 0.0, NEG_FILL, product))
            jobs.append((u, j, h, query_live))
    tops = [jnp.max(s, axis=1, keepdims=True) for s in scores]
    weights = [jnp.exp2((s - m) * EXP_SCALE) for s, m in zip(scores, tops)]
    totals = [jnp.sum(w, axis=1, keepdims=True) for w in weights]
    for (u, j, h, query_live), w, total in zip(jobs, weights, totals):
        v = line[u, :, 2 * width + h * HD : 2 * width + (h + 1) * HD]
        added = lax.dot_general(
            w.astype(jnp.bfloat16), v, (((1,), (0,)), ((), ())), preferred_element_type=jnp.float32
        )
        safe = jnp.where(query_live, total, 1.0)
        done = jnp.where(query_live, added / safe, 0.0)
        held[h, pl.ds(j, cells, stride=own), :] = done

    @pl.when(step == pl.num_programs(0) - 1)
    def _():
        for s in range(peers):
            at = pl.multiple_of((me ^ s) * span * own, span * own)
            for h in range(HC):
                part = held[h, pl.ds(at, span * own), :].reshape(span, own, HD)
                outs[s][:, :, h * HD : (h + 1) * HD] = part.astype(jnp.bfloat16)


def col_attend(me, pattern, count, pieces):
    peers = len(pieces)
    own, span, wide = pieces[0].shape
    width = HC * HD
    chosen = pattern.shape[-1]
    lines = 2
    result = (span, own, width)
    return pl.pallas_call(
        functools.partial(col_attend_kernel, chosen=chosen, lines=lines),
        grid_spec=pltpu.PrefetchScalarGridSpec(
            num_scalar_prefetch=3,
            grid=(own // lines,),
            in_specs=[pl.BlockSpec(memory_space=pltpu.VMEM)] * peers,
            out_specs=[pl.BlockSpec(result, lambda j, *_: (0, 0, 0))] * peers,
            scratch_shapes=[
                pltpu.VMEM((lines, peers * span, wide), jnp.bfloat16),
                pltpu.VMEM((HC, own * peers * span, HD), jnp.float32),
            ],
        ),
        out_shape=[jax.ShapeDtypeStruct(result, jnp.bfloat16)] * peers,
        compiler_params=grant(56),
        name="col_attend",
    )(me, pattern.reshape(-1), count, pieces[0], *[in_place(p) for p in pieces[1:]])


def project_kernel(place, row_ref, *rest, peers, near):
    pieces, (out_ref, heads, line, sem) = rest[:peers], rest[-4:]
    weights = rest[peers:-4]
    width = HR * HD
    own = pieces[0].shape[1]
    me, plane = place[0], place[1]
    step = pl.program_id(0)
    slot = lax.rem(step, 2)
    at_x, at_z = lax.div(plane, near), lax.rem(plane, near)

    def fetch(step, slot):
        turn = lax.rem(step, near)
        for core in range(2):

            @pl.when(lax.div(step, near) == core)
            def _(core=core):
                group = weights[2 * near * core : 2 * near * (core + 1)]
                for a in range(near):
                    for b in range(near):
                        for half, (x, z) in enumerate(((a, b), (b, a))):
                            source = group[half * near + a].at[b, turn]
                            span, wide = source.shape
                            at = ((at_x ^ x) * near + (at_z ^ z)) * span
                            target = line.at[
                                slot,
                                pl.ds(pl.multiple_of(at, span), span),
                                pl.ds(half * wide, wide),
                            ]
                            pltpu.make_async_copy(source, target, sem.at[slot]).start()

    @pl.when(step == 0)
    def _():
        fetch(step, slot)
        odd = lax.rem(me, 2) == 1
        heads[:, :, 0:width] = row_ref[...]
        for s in range(0, peers, 2):
            a = pieces[s][...].astype(jnp.float32)
            b = pieces[s + 1][...].astype(jnp.float32)
            both = jnp.concatenate([jnp.where(odd, b, a), jnp.where(odd, a, b)], axis=1)
            at = pl.multiple_of(((me ^ s) // 2) * 2 * own, 2 * own)
            heads[:, pl.ds(at, 2 * own), width:] = both.astype(jnp.bfloat16)

    @pl.when(step + 1 < pl.num_programs(0))
    def _():
        fetch(step + 1, 1 - slot)

    pltpu.make_async_copy(line.at[slot], line.at[slot], sem.at[slot]).wait()
    out_ref[...] = lax.dot_general(
        heads[...].reshape(-1, heads.shape[2]),
        line[slot],
        (((1,), (1,)), ((), ())),
        preferred_element_type=jnp.float32,
    ).astype(jnp.bfloat16)


def project(place, row_out, pieces, weights, outs):
    span, cells, _ = row_out.shape
    turns, near, part, wide = weights[0].shape
    channels = 2 * wide
    tile = near * near * part
    held = pl.BlockSpec(memory_space=pltpu.VMEM)

    def target(j, at):
        return 0, at[0] ^ (2 * lax.rem(j, turns) + lax.div(j, turns))

    return pl.pallas_call(
        functools.partial(project_kernel, peers=len(pieces), near=near),
        grid_spec=pltpu.PrefetchScalarGridSpec(
            num_scalar_prefetch=1,
            grid=(2 * turns,),
            in_specs=[held] * (1 + len(pieces))
            + [pl.BlockSpec(memory_space=pl.ANY)] * len(weights),
            out_specs=pl.BlockSpec((span * cells, tile), target),
            scratch_shapes=[
                pltpu.VMEM((span, cells, channels), jnp.bfloat16),
                pltpu.VMEM((2, tile, channels), jnp.bfloat16),
                pltpu.SemaphoreType.DMA((2,)),
            ],
        ),
        out_shape=jax.ShapeDtypeStruct((span * cells, outs), jnp.bfloat16),
        compiler_params=grant(56),
        name="project",
    )(place, in_place(row_out), pieces[0], *[in_place(p) for p in pieces[1:]], *weights)


def by_xor(x, axis, masks):
    size = lax.axis_size(axis)
    return [lax.ppermute(x, axis, [(d, d ^ s) for d in range(size)]) for s in masks]


def swap_pieces(pieces):
    peers = len(pieces)
    return [pieces[0]] + [
        lax.ppermute(pieces[s], "rows", [(d, d ^ s) for d in range(peers)])
        for s in range(1, peers)
    ]


def halve_kernel(*refs):
    parts, (upper, lower) = refs[:-2], refs[-2:]
    middle = upper.shape[2]
    for i, part in enumerate(parts):
        upper[i] = part[:, :middle]
        lower[i] = part[:, middle:]


def halve(parts):
    span, channels = parts[0].shape
    half = jax.ShapeDtypeStruct((len(parts), span, channels // 2), parts[0].dtype)
    held = pl.BlockSpec(memory_space=pltpu.VMEM)
    return pl.pallas_call(
        halve_kernel,
        in_specs=[held] * len(parts),
        out_specs=[held, held],
        out_shape=[half, half],
        compiler_params=grant(56),
        name="halve",
    )(parts[0], *[in_place(p) for p in parts[1:]])


def body(
    query_cells, key_cells, value_cells, out_weight, row_pattern, row_count, col_pattern, col_count
):
    row_span, col_span, _ = query_cells.shape
    peers = lax.axis_size("rows")
    row_share = row_span // lax.axis_size("cols")
    me = lax.axis_index("rows").astype(jnp.int32).reshape(1)
    row_first = lax.axis_index("cols") * row_share
    pattern = lax.dynamic_slice_in_dim(row_pattern, row_first, row_share, 0)
    count = lax.dynamic_slice_in_dim(row_count, row_first, row_share, 0)

    place = jnp.stack([lax.axis_index("rows"), lax.axis_index("cols")]).astype(jnp.int32)

    shard = out_weight.T
    packed = row_pack(query_cells, key_cells, value_cells)
    lines = lax.all_to_all(packed, "cols", 0, 0, tiled=True)
    along_y = [shard] + by_xor(shard, "rows", (2, 4, 6))
    sent = col_pack(me, query_cells, key_cells, value_cells, peers)
    pieces = swap_pieces(sent)
    upper, lower = halve(along_y)
    along_z = [upper] + by_xor(upper, "cols", (1, 2, 3))
    along_x = [lower] + by_xor(lower, "cols", (4, 8, 12))
    upper, lower = jnp.stack(along_z), jnp.stack(along_x)
    weights = [upper] + by_xor(upper, "cols", (4, 8, 12))
    weights += [lower] + by_xor(lower, "cols", (1, 2, 3))
    row_out = row_attend(pattern, count, lines)
    row_out = lax.all_to_all(row_out.reshape(row_span, col_span, -1), "cols", 0, 0, tiled=True)
    col_out = col_attend(me, col_pattern, col_count, pieces)
    col_out = swap_pieces(col_out)
    weights += [by_xor(w, "rows", (1,))[0] for w in weights]
    outs = out_weight.shape[1] * peers * lax.axis_size("cols")
    projected = project(place, row_out, col_out, weights, outs)
    return projected.reshape(row_span, col_span, projected.shape[-1])


def solution(mesh):
    placed = (
        P("rows", "cols", None),
        P("rows", "cols", None),
        P("rows", "cols", None),
        P(None, ("rows", "cols")),
        P("rows", None, None),
        P("rows"),
        P("cols", None, None),
        P("cols"),
    )
    return jax.shard_map(
        body, mesh=mesh, in_specs=placed, out_specs=P("rows", "cols", None), check_vma=False
    )
```

```python
import functools
import math

import jax
import jax.numpy as jnp
from jax import lax
from jax.experimental import pallas as pl
from jax.experimental.pallas import tpu as pltpu
from jax.sharding import PartitionSpec as P


HR = 4
HC = 4
HD = 128
BLK = 32
NEG_FILL = -1e30
UNROLL = 4
EXP_SCALE = HD ** (-0.5) * math.log2(math.e)


def grant(mebibytes):
    return pltpu.CompilerParams(vmem_limit_bytes=mebibytes << 20)


def in_place(x):
    return pltpu.with_memory_space_constraint(x, pltpu.VMEM)


def row_pack_kernel(q_ref, k_ref, v_ref, out_ref):
    width = HR * HD
    out_ref[:, :, 0:width] = q_ref[...]
    out_ref[:, :, width : 2 * width] = k_ref[...]
    out_ref[:, :, 2 * width : 3 * width] = v_ref[...]


def row_pack(q, k, v):
    span, cells, _ = q.shape
    width = HR * HD
    step = 4
    part = pl.BlockSpec((step, cells, width), lambda i: (i, 0, 0))
    return pl.pallas_call(
        row_pack_kernel,
        grid=(span // step,),
        in_specs=[part, part, part],
        out_specs=pl.BlockSpec((step, cells, 3 * width), lambda i: (i, 0, 0)),
        out_shape=jax.ShapeDtypeStruct((span, cells, 3 * width), q.dtype),
        compiler_params=grant(56),
        name="row_pack",
    )(q, k, v)


def col_pack_kernel(me_ref, q_ref, k_ref, v_ref, *rest):
    outs, (wide, buf, sem) = rest[:-3], rest[-3:]
    peers = len(outs)
    width = HC * HD
    span, own, _ = q_ref.shape
    step = pl.program_id(0)
    slot = lax.rem(step, 2)

    @pl.when(step >= 2)
    def _():
        pltpu.make_async_copy(buf.at[slot], outs[0], sem.at[slot]).wait()

    for t, ref in enumerate((q_ref, k_ref, v_ref)):
        for h in range(HC):
            lanes = slice(h * HD, (h + 1) * HD)
            wide[t * HC + h] = ref[:, :, lanes].reshape(span * own, HD).astype(jnp.float32)
    for t in range(3):
        for h in range(HC):
            for j in range(own):
                line = wide[t * HC + h, pl.ds(j, span, stride=own), :]
                at = t * width + h * HD
                buf[slot, j, :, at : at + HD] = line.astype(jnp.bfloat16)
    for s in range(peers):

        @pl.when(step == s)
        def _(s=s):
            pltpu.make_async_copy(buf.at[slot], outs[s], sem.at[slot]).start()

    @pl.when(step == peers - 1)
    def _():
        pltpu.make_async_copy(buf.at[1 - slot], outs[0], sem.at[1 - slot]).wait()
        pltpu.make_async_copy(buf.at[slot], outs[0], sem.at[slot]).wait()


def col_pack(me, q, k, v, peers):
    span, cells, _ = q.shape
    width = HC * HD
    own = cells // peers
    part = pl.BlockSpec((span, own, width), lambda s, me: (0, me[0] ^ s, 1))
    piece = (own, span, 3 * width)
    return pl.pallas_call(
        col_pack_kernel,
        grid_spec=pltpu.PrefetchScalarGridSpec(
            num_scalar_prefetch=1,
            grid=(peers,),
            in_specs=[part, part, part],
            out_specs=[pl.BlockSpec(memory_space=pl.ANY)] * peers,
            scratch_shapes=[
                pltpu.VMEM((3 * HC, span * own, HD), jnp.float32),
                pltpu.VMEM((2,) + piece, q.dtype),
                pltpu.SemaphoreType.DMA((2,)),
            ],
        ),
        out_shape=[jax.ShapeDtypeStruct(piece, q.dtype)] * peers,
        compiler_params=grant(56),
        name="col_pack",
    )(me, q, k, v)


def row_attend_kernel(pattern_ref, count_ref, x_ref, out_ref, *, chosen):
    width = HR * HD
    count = count_ref[0]
    per = x_ref.shape[1] // BLK
    blocks = x_ref.shape[0] * per
    key_lane = lax.broadcasted_iota(jnp.int32, (1, chosen * BLK), 1)
    slot_of = key_lane // BLK
    in_block = key_lane - slot_of * BLK
    query_row = lax.broadcasted_iota(jnp.int32, (BLK, 1), 0)
    zero = jnp.zeros((BLK, HD), jnp.bfloat16)

    def block(b, lanes):
        at = pl.multiple_of(lax.rem(b, per) * BLK, BLK)
        return x_ref[lax.div(b, per), pl.ds(at, BLK), lanes]

    def stage_scores(n):
        q = block(n, slice(0, width))
        keys = []
        limit = jnp.zeros((1, chosen * BLK), jnp.int32)
        for s in range(chosen):
            b = pattern_ref[n * chosen + s]
            keys.append(block(b, slice(width, 2 * width)))
            limit = jnp.where(slot_of == s, count - b * BLK, limit)
        keys = jnp.concatenate(keys, axis=0)
        live = in_block < limit
        spread = jnp.concatenate(
            [
                jnp.concatenate(
                    [q[:, h * HD : (h + 1) * HD] if g == h else zero for g in range(HR)], axis=1
                )
                for h in range(HR)
            ],
            axis=0,
        )
        scores = lax.dot_general(
            spread, keys, (((1,), (1,)), ((), ())), preferred_element_type=jnp.float32
        )
        return jnp.where(live, scores, NEG_FILL)

    def stage_values(n, weights, total):
        at = pl.multiple_of(n * BLK, BLK)
        values = []
        for s in range(chosen):
            values.append(block(pattern_ref[n * chosen + s], slice(2 * width, 3 * width)))
        values = jnp.concatenate(values, axis=0)
        query_live = (query_row + n * BLK) < count
        for pair in range(HR // 2):
            rows = slice(pair * 2 * BLK, (pair + 1) * 2 * BLK)
            lanes = slice(pair * 2 * HD, (pair + 1) * 2 * HD)
            added = lax.dot_general(
                weights[rows],
                values[:, lanes],
                (((1,), (0,)), ((), ())),
                preferred_element_type=jnp.float32,
            )
            for g in range(2):
                h = pair * 2 + g
                part = added[g * BLK : (g + 1) * BLK, g * HD : (g + 1) * HD]
                safe = jnp.where(query_live, total[h * BLK : (h + 1) * BLK], 1.0)
                done = jnp.where(query_live, part / safe, 0.0)
                out_ref[pl.ds(at, BLK), h * HD : (h + 1) * HD] = done.astype(jnp.bfloat16)

    def group(g, _):
        blocks_here = [g * UNROLL + u for u in range(UNROLL)]
        scores = [stage_scores(n) for n in blocks_here]
        tops = [jnp.max(s, axis=1, keepdims=True) for s in scores]
        weights = [jnp.exp2((s - m) * EXP_SCALE) for s, m in zip(scores, tops)]
        totals = [jnp.sum(w, axis=1, keepdims=True) for w in weights]
        for n, w, t in zip(blocks_here, weights, totals):
            stage_values(n, w.astype(jnp.bfloat16), t)
        return 0

    lax.fori_loop(0, blocks // UNROLL, group, 0)


def row_attend(pattern, count, x):
    cells = x.shape[0] * x.shape[1]
    chosen = pattern.shape[-1]
    return pl.pallas_call(
        functools.partial(row_attend_kernel, chosen=chosen),
        grid_spec=pltpu.PrefetchScalarGridSpec(
            num_scalar_prefetch=2,
            grid=(1,),
            in_specs=[pl.BlockSpec(memory_space=pltpu.VMEM)],
            out_specs=pl.BlockSpec((cells, HR * HD), lambda i, *_: (0, 0)),
        ),
        out_shape=jax.ShapeDtypeStruct((cells, HR * HD), x.dtype),
        compiler_params=grant(56),
        name="row_attend",
    )(pattern.reshape(-1), count, in_place(x))


def col_attend_kernel(me_ref, pattern_ref, count_ref, *rest, chosen, lines):
    peers = (len(rest) - 2) // 2
    pieces, outs, (line, held) = rest[:peers], rest[peers : 2 * peers], rest[2 * peers :]
    width = HC * HD
    me = me_ref[0]
    step = pl.program_id(0)
    span = pieces[0].shape[1]
    cells = peers * span
    own = held.shape[1] // cells
    blocks = cells // BLK
    key_at = lax.broadcasted_iota(jnp.int32, (1, cells), 1)
    key_block = key_at // BLK
    query_row = lax.broadcasted_iota(jnp.int32, (cells, 1), 0)
    for u in range(lines):
        for s in range(peers):
            line[u, pl.ds(pl.multiple_of((me ^ s) * span, span), span), :] = pieces[s][step * lines + u]
    jobs, scores = [], []
    for u in range(lines):
        j = step * lines + u
        first = me * own + j
        count = count_ref[first]
        rows = []
        for n in range(blocks):
            listed = key_block == pattern_ref[(first * blocks + n) * chosen]
            for s in range(1, chosen):
                listed = listed | (key_block == pattern_ref[(first * blocks + n) * chosen + s])
            row = jnp.where(listed & (key_at < count), 0.0, NEG_FILL)
            rows.append(jnp.broadcast_to(row, (BLK, cells)))
        bias = jnp.concatenate(rows, axis=0)
        query_live = query_row < count
        for h in range(HC):
            q = line[u, :, h * HD : (h + 1) * HD]
            k = line[u, :, width + h * HD : width + (h + 1) * HD]
            product = lax.dot_general(
                q, k, (((1,), (1,)), ((), ())), preferred_element_type=jnp.float32
            )
            scores.append(jnp.where(bias < 0.0, NEG_FILL, product))
            jobs.append((u, j, h, query_live))
    tops = [jnp.max(s, axis=1, keepdims=True) for s in scores]
    weights = [jnp.exp2((s - m) * EXP_SCALE) for s, m in zip(scores, tops)]
    totals = [jnp.sum(w, axis=1, keepdims=True) for w in weights]
    for (u, j, h, query_live), w, total in zip(jobs, weights, totals):
        v = line[u, :, 2 * width + h * HD : 2 * width + (h + 1) * HD]
        added = lax.dot_general(
            w.astype(jnp.bfloat16), v, (((1,), (0,)), ((), ())), preferred_element_type=jnp.float32
        )
        safe = jnp.where(query_live, total, 1.0)
        done = jnp.where(query_live, added / safe, 0.0)
        held[h, pl.ds(j, cells, stride=own), :] = done

    @pl.when(step == pl.num_programs(0) - 1)
    def _():
        for s in range(peers):
            at = pl.multiple_of((me ^ s) * span * own, span * own)
            for h in range(HC):
                part = held[h, pl.ds(at, span * own), :].reshape(span, own, HD)
                outs[s][:, :, h * HD : (h + 1) * HD] = part.astype(jnp.bfloat16)


def col_attend(me, pattern, count, pieces):
    peers = len(pieces)
    own, span, wide = pieces[0].shape
    width = HC * HD
    chosen = pattern.shape[-1]
    lines = 2
    result = (span, own, width)
    return pl.pallas_call(
        functools.partial(col_attend_kernel, chosen=chosen, lines=lines),
        grid_spec=pltpu.PrefetchScalarGridSpec(
            num_scalar_prefetch=3,
            grid=(own // lines,),
            in_specs=[pl.BlockSpec(memory_space=pltpu.VMEM)] * peers,
            out_specs=[pl.BlockSpec(result, lambda j, *_: (0, 0, 0))] * peers,
            scratch_shapes=[
                pltpu.VMEM((lines, peers * span, wide), jnp.bfloat16),
                pltpu.VMEM((HC, own * peers * span, HD), jnp.float32),
            ],
        ),
        out_shape=[jax.ShapeDtypeStruct(result, jnp.bfloat16)] * peers,
        compiler_params=grant(56),
        name="col_attend",
    )(me, pattern.reshape(-1), count, pieces[0], *[in_place(p) for p in pieces[1:]])


def fetch_weights(plane, weights, line, sem, step, slot, flipped):
    near = weights[0].shape[0]
    at_x, at_z = lax.div(plane, near), lax.rem(plane, near)
    turn = lax.rem(step, near)
    for core in range(2):

        @pl.when(lax.div(step, near) == core)
        def _(core=core):
            for a in range(near):
                for b in range(near):
                    x, z = (b, a) if flipped else (a, b)
                    source = weights[core * near + a].at[b, turn]
                    span = source.shape[0]
                    at = pl.multiple_of(((at_x ^ x) * near + (at_z ^ z)) * span, span)
                    target = line.at[slot, pl.ds(at, span), :]
                    pltpu.make_async_copy(source, target, sem.at[slot]).start()


def project_step(plane, weights, line, sem, flipped, heads):
    step = pl.program_id(0)
    slot = lax.rem(step, 2)

    @pl.when(step == 0)
    def _():
        fetch_weights(plane, weights, line, sem, step, slot, flipped)

    @pl.when(step + 1 < pl.num_programs(0))
    def _():
        fetch_weights(plane, weights, line, sem, step + 1, 1 - slot, flipped)

    pltpu.make_async_copy(line.at[slot], line.at[slot], sem.at[slot]).wait()
    return lax.dot_general(
        heads[...].reshape(-1, heads.shape[2]),
        line[slot],
        (((1,), (1,)), ((), ())),
        preferred_element_type=jnp.float32,
    )


def project_rows_kernel(place, heads, *rest):
    weights, (out_ref, line, sem) = rest[:-3], rest[-3:]
    out_ref[...] = project_step(place[1], weights, line, sem, False, heads)


def project_cols_kernel(place, *rest, peers):
    pieces, weights = rest[:peers], rest[peers:-5]
    partial_ref, out_ref, heads, line, sem = rest[-5:]
    own = pieces[0].shape[1]

    @pl.when(pl.program_id(0) == 0)
    def _():
        me = place[0]
        odd = lax.rem(me, 2) == 1
        for s in range(0, peers, 2):
            a = pieces[s][...].astype(jnp.float32)
            b = pieces[s + 1][...].astype(jnp.float32)
            both = jnp.concatenate([jnp.where(odd, b, a), jnp.where(odd, a, b)], axis=1)
            at = pl.multiple_of(((me ^ s) // 2) * 2 * own, 2 * own)
            heads[:, pl.ds(at, 2 * own), :] = both.astype(jnp.bfloat16)

    added = project_step(place[1], weights, line, sem, True, heads)
    out_ref[...] = (partial_ref[...] + added).astype(jnp.bfloat16)


def project_sizes(weights):
    near, turns, part, width = weights[0].shape
    tile = near * near * part

    def target(j, at):
        return 0, at[0] ^ (2 * lax.rem(j, turns) + lax.div(j, turns))

    scratch = [pltpu.VMEM((2, tile, width), jnp.bfloat16), pltpu.SemaphoreType.DMA((2,))]
    return 2 * turns, tile, target, scratch


def project_rows(place, row_out, weights, outs):
    span, cells, _ = row_out.shape
    steps, tile, target, scratch = project_sizes(weights)
    return pl.pallas_call(
        project_rows_kernel,
        grid_spec=pltpu.PrefetchScalarGridSpec(
            num_scalar_prefetch=1,
            grid=(steps,),
            in_specs=[pl.BlockSpec(memory_space=pltpu.VMEM)]
            + [pl.BlockSpec(memory_space=pl.ANY)] * len(weights),
            out_specs=pl.BlockSpec((span * cells, tile), target),
            scratch_shapes=scratch,
        ),
        out_shape=jax.ShapeDtypeStruct((span * cells, outs), jnp.float32),
        compiler_params=grant(56),
        name="project_rows",
    )(place, in_place(row_out), *weights)


def project_cols(place, pieces, weights, partial):
    span, own, width = pieces[0].shape
    steps, tile, target, scratch = project_sizes(weights)
    block = pl.BlockSpec((partial.shape[0], tile), target)
    return pl.pallas_call(
        functools.partial(project_cols_kernel, peers=len(pieces)),
        grid_spec=pltpu.PrefetchScalarGridSpec(
            num_scalar_prefetch=1,
            grid=(steps,),
            in_specs=[pl.BlockSpec(memory_space=pltpu.VMEM)] * len(pieces)
            + [pl.BlockSpec(memory_space=pl.ANY)] * len(weights)
            + [block],
            out_specs=block,
            scratch_shapes=[pltpu.VMEM((span, own * len(pieces), width), jnp.bfloat16)] + scratch,
        ),
        out_shape=jax.ShapeDtypeStruct(partial.shape, jnp.bfloat16),
        compiler_params=grant(56),
        name="project_cols",
    )(place, pieces[0], *[in_place(p) for p in pieces[1:]], *weights, partial)


def by_xor(x, axis, masks):
    size = lax.axis_size(axis)
    return [lax.ppermute(x, axis, [(d, d ^ s) for d in range(size)]) for s in masks]


def swap_pieces(pieces):
    peers = len(pieces)
    return [pieces[0]] + [
        lax.ppermute(pieces[s], "rows", [(d, d ^ s) for d in range(peers)])
        for s in range(1, peers)
    ]


def join_kernel(*refs):
    parts, outs = refs[:-2], refs[-2:]
    each = len(parts) // 2
    for i, part in enumerate(parts):
        outs[i // each][i % each] = part[...]


def join_both(first, second):
    held = pl.BlockSpec(memory_space=pltpu.VMEM)
    whole = jax.ShapeDtypeStruct((len(first),) + first[0].shape, first[0].dtype)
    return pl.pallas_call(
        join_kernel,
        in_specs=[held] * (len(first) + len(second)),
        out_specs=[held, held],
        out_shape=[whole, whole],
        compiler_params=grant(56),
        name="join_both",
    )(*[in_place(p) for p in first], *[in_place(p) for p in second])


def halve_kernel(*refs):
    parts, (upper, lower) = refs[:-2], refs[-2:]
    middle = upper.shape[2]
    for i, part in enumerate(parts):
        upper[i] = part[:, :middle]
        lower[i] = part[:, middle:]


def halve(parts):
    span, channels = parts[0].shape
    half = jax.ShapeDtypeStruct((len(parts), span, channels // 2), parts[0].dtype)
    held = pl.BlockSpec(memory_space=pltpu.VMEM)
    return pl.pallas_call(
        halve_kernel,
        in_specs=[held] * len(parts),
        out_specs=[held, held],
        out_shape=[half, half],
        compiler_params=grant(56),
        name="halve",
    )(parts[0], *[in_place(p) for p in parts[1:]])


def body(
    query_cells, key_cells, value_cells, out_weight, row_pattern, row_count, col_pattern, col_count
):
    row_span, col_span, _ = query_cells.shape
    peers = lax.axis_size("rows")
    row_share = row_span // lax.axis_size("cols")
    me = lax.axis_index("rows").astype(jnp.int32).reshape(1)
    row_first = lax.axis_index("cols") * row_share
    pattern = lax.dynamic_slice_in_dim(row_pattern, row_first, row_share, 0)
    count = lax.dynamic_slice_in_dim(row_count, row_first, row_share, 0)

    place = jnp.stack([lax.axis_index("rows"), lax.axis_index("cols")]).astype(jnp.int32)

    shard = out_weight.T
    packed = row_pack(query_cells, key_cells, value_cells)
    lines = lax.all_to_all(packed, "cols", 0, 0, tiled=True)
    along_y = [shard] + by_xor(shard, "rows", (2, 4, 6))
    sent = col_pack(me, query_cells, key_cells, value_cells, peers)
    pieces = swap_pieces(sent)
    upper, lower = halve(along_y)
    along_z = [upper] + by_xor(upper, "cols", (1, 2, 3))
    along_x = [lower] + by_xor(lower, "cols", (4, 8, 12))
    upper, lower = join_both(along_z, along_x)
    uppers = [upper] + by_xor(upper, "cols", (4, 8, 12))
    lowers = [lower] + by_xor(lower, "cols", (1, 2, 3))
    row_out = row_attend(pattern, count, lines)
    row_out = lax.all_to_all(row_out.reshape(row_span, col_span, -1), "cols", 0, 0, tiled=True)
    col_out = col_attend(me, col_pattern, col_count, pieces)
    col_out = swap_pieces(col_out)
    uppers += [by_xor(w, "rows", (1,))[0] for w in uppers]
    lowers += [by_xor(w, "rows", (1,))[0] for w in lowers]
    outs = out_weight.shape[1] * peers * lax.axis_size("cols")
    partial = project_rows(place, row_out, uppers, outs)
    projected = project_cols(place, col_out, lowers, partial)
    return projected.reshape(row_span, col_span, projected.shape[-1])


def solution(mesh):
    placed = (
        P("rows", "cols", None),
        P("rows", "cols", None),
        P("rows", "cols", None),
        P(None, ("rows", "cols")),
        P("rows", None, None),
        P("rows"),
        P("cols", None, None),
        P("cols"),
    )
    return jax.shard_map(
        body, mesh=mesh, in_specs=placed, out_specs=P("rows", "cols", None), check_vma=False
    )
```

```python
import functools
import math

import jax
import jax.numpy as jnp
from jax import lax
from jax.experimental import pallas as pl
from jax.experimental.pallas import tpu as pltpu
from jax.sharding import PartitionSpec as P


HR = 4
HC = 4
HD = 128
BLK = 32
NEG_FILL = -1e30
UNROLL = 4
EXP_SCALE = HD ** (-0.5) * math.log2(math.e)


def grant(mebibytes):
    return pltpu.CompilerParams(vmem_limit_bytes=mebibytes << 20)


def in_place(x):
    return pltpu.with_memory_space_constraint(x, pltpu.VMEM)


def row_pack_kernel(q_ref, k_ref, v_ref, out_ref):
    width = HR * HD
    out_ref[:, :, 0:width] = q_ref[...]
    out_ref[:, :, width : 2 * width] = k_ref[...]
    out_ref[:, :, 2 * width : 3 * width] = v_ref[...]


def row_pack(q, k, v):
    span, cells, _ = q.shape
    width = HR * HD
    step = 4
    part = pl.BlockSpec((step, cells, width), lambda i: (i, 0, 0))
    return pl.pallas_call(
        row_pack_kernel,
        grid=(span // step,),
        in_specs=[part, part, part],
        out_specs=pl.BlockSpec((step, cells, 3 * width), lambda i: (i, 0, 0)),
        out_shape=jax.ShapeDtypeStruct((span, cells, 3 * width), q.dtype),
        compiler_params=grant(56),
        name="row_pack",
    )(q, k, v)


def col_pack_kernel(me_ref, q_ref, k_ref, v_ref, *rest):
    outs, (wide, buf, sem) = rest[:-3], rest[-3:]
    peers = len(outs)
    width = HC * HD
    span, own, _ = q_ref.shape
    step = pl.program_id(0)
    slot = lax.rem(step, 2)

    @pl.when(step >= 2)
    def _():
        pltpu.make_async_copy(buf.at[slot], outs[0], sem.at[slot]).wait()

    for t, ref in enumerate((q_ref, k_ref, v_ref)):
        for h in range(HC):
            lanes = slice(h * HD, (h + 1) * HD)
            wide[t * HC + h] = ref[:, :, lanes].reshape(span * own, HD).astype(jnp.float32)
    for t in range(3):
        for h in range(HC):
            for j in range(own):
                line = wide[t * HC + h, pl.ds(j, span, stride=own), :]
                at = t * width + h * HD
                buf[slot, j, :, at : at + HD] = line.astype(jnp.bfloat16)
    for s in range(peers):

        @pl.when(step == s)
        def _(s=s):
            pltpu.make_async_copy(buf.at[slot], outs[s], sem.at[slot]).start()

    @pl.when(step == peers - 1)
    def _():
        pltpu.make_async_copy(buf.at[1 - slot], outs[0], sem.at[1 - slot]).wait()
        pltpu.make_async_copy(buf.at[slot], outs[0], sem.at[slot]).wait()


def col_pack(me, q, k, v, peers):
    span, cells, _ = q.shape
    width = HC * HD
    own = cells // peers
    part = pl.BlockSpec((span, own, width), lambda s, me: (0, me[0] ^ s, 1))
    piece = (own, span, 3 * width)
    return pl.pallas_call(
        col_pack_kernel,
        grid_spec=pltpu.PrefetchScalarGridSpec(
            num_scalar_prefetch=1,
            grid=(peers,),
            in_specs=[part, part, part],
            out_specs=[pl.BlockSpec(memory_space=pl.ANY)] * peers,
            scratch_shapes=[
                pltpu.VMEM((3 * HC, span * own, HD), jnp.float32),
                pltpu.VMEM((2,) + piece, q.dtype),
                pltpu.SemaphoreType.DMA((2,)),
            ],
        ),
        out_shape=[jax.ShapeDtypeStruct(piece, q.dtype)] * peers,
        compiler_params=grant(56),
        name="col_pack",
    )(me, q, k, v)


def row_attend_kernel(pattern_ref, count_ref, x_ref, out_ref, *, chosen):
    width = HR * HD
    count = count_ref[0]
    per = x_ref.shape[1] // BLK
    blocks = x_ref.shape[0] * per
    key_lane = lax.broadcasted_iota(jnp.int32, (1, chosen * BLK), 1)
    slot_of = key_lane // BLK
    in_block = key_lane - slot_of * BLK
    query_row = lax.broadcasted_iota(jnp.int32, (BLK, 1), 0)
    zero = jnp.zeros((BLK, HD), jnp.bfloat16)

    def block(b, lanes):
        at = pl.multiple_of(lax.rem(b, per) * BLK, BLK)
        return x_ref[lax.div(b, per), pl.ds(at, BLK), lanes]

    def stage_scores(n):
        q = block(n, slice(0, width))
        keys = []
        limit = jnp.zeros((1, chosen * BLK), jnp.int32)
        for s in range(chosen):
            b = pattern_ref[n * chosen + s]
            keys.append(block(b, slice(width, 2 * width)))
            limit = jnp.where(slot_of == s, count - b * BLK, limit)
        keys = jnp.concatenate(keys, axis=0)
        live = in_block < limit
        spread = jnp.concatenate(
            [
                jnp.concatenate(
                    [q[:, h * HD : (h + 1) * HD] if g == h else zero for g in range(HR)], axis=1
                )
                for h in range(HR)
            ],
            axis=0,
        )
        scores = lax.dot_general(
            spread, keys, (((1,), (1,)), ((), ())), preferred_element_type=jnp.float32
        )
        return jnp.where(live, scores, NEG_FILL)

    def stage_values(n, weights, total):
        at = pl.multiple_of(n * BLK, BLK)
        values = []
        for s in range(chosen):
            values.append(block(pattern_ref[n * chosen + s], slice(2 * width, 3 * width)))
        values = jnp.concatenate(values, axis=0)
        query_live = (query_row + n * BLK) < count
        for pair in range(HR // 2):
            rows = slice(pair * 2 * BLK, (pair + 1) * 2 * BLK)
            lanes = slice(pair * 2 * HD, (pair + 1) * 2 * HD)
            added = lax.dot_general(
                weights[rows],
                values[:, lanes],
                (((1,), (0,)), ((), ())),
                preferred_element_type=jnp.float32,
            )
            for g in range(2):
                h = pair * 2 + g
                part = added[g * BLK : (g + 1) * BLK, g * HD : (g + 1) * HD]
                safe = jnp.where(query_live, total[h * BLK : (h + 1) * BLK], 1.0)
                done = jnp.where(query_live, part / safe, 0.0)
                out_ref[pl.ds(at, BLK), h * HD : (h + 1) * HD] = done.astype(jnp.bfloat16)

    def group(g, _):
        blocks_here = [g * UNROLL + u for u in range(UNROLL)]
        scores = [stage_scores(n) for n in blocks_here]
        tops = [jnp.max(s, axis=1, keepdims=True) for s in scores]
        weights = [jnp.exp2((s - m) * EXP_SCALE) for s, m in zip(scores, tops)]
        totals = [jnp.sum(w, axis=1, keepdims=True) for w in weights]
        for n, w, t in zip(blocks_here, weights, totals):
            stage_values(n, w.astype(jnp.bfloat16), t)
        return 0

    lax.fori_loop(0, blocks // UNROLL, group, 0)


def row_attend(pattern, chosen, count, x):
    cells = x.shape[0] * x.shape[1]
    return pl.pallas_call(
        functools.partial(row_attend_kernel, chosen=chosen),
        grid_spec=pltpu.PrefetchScalarGridSpec(
            num_scalar_prefetch=2,
            grid=(1,),
            in_specs=[pl.BlockSpec(memory_space=pltpu.VMEM)],
            out_specs=pl.BlockSpec((cells, HR * HD), lambda i, *_: (0, 0)),
        ),
        out_shape=jax.ShapeDtypeStruct((cells, HR * HD), x.dtype),
        compiler_params=grant(56),
        name="row_attend",
    )(pattern, count, in_place(x))


def col_attend_kernel(me_ref, pattern_ref, count_ref, *rest, chosen, lines):
    peers = (len(rest) - 2) // 2
    pieces, outs, (line, held) = rest[:peers], rest[peers : 2 * peers], rest[2 * peers :]
    width = HC * HD
    me = me_ref[0]
    step = pl.program_id(0)
    span = pieces[0].shape[1]
    cells = peers * span
    own = held.shape[1] // cells
    blocks = cells // BLK
    key_at = lax.broadcasted_iota(jnp.int32, (1, cells), 1)
    key_block = key_at // BLK
    query_row = lax.broadcasted_iota(jnp.int32, (cells, 1), 0)
    for u in range(lines):
        for s in range(peers):
            line[u, pl.ds(pl.multiple_of((me ^ s) * span, span), span), :] = pieces[s][step * lines + u]
    jobs, scores = [], []
    for u in range(lines):
        j = step * lines + u
        first = me * own + j
        count = count_ref[first]
        rows = []
        for n in range(blocks):
            listed = key_block == pattern_ref[(first * blocks + n) * chosen]
            for s in range(1, chosen):
                listed = listed | (key_block == pattern_ref[(first * blocks + n) * chosen + s])
            row = jnp.where(listed & (key_at < count), 0.0, NEG_FILL)
            rows.append(jnp.broadcast_to(row, (BLK, cells)))
        bias = jnp.concatenate(rows, axis=0)
        query_live = query_row < count
        for h in range(HC):
            q = line[u, :, h * HD : (h + 1) * HD]
            k = line[u, :, width + h * HD : width + (h + 1) * HD]
            product = lax.dot_general(
                q, k, (((1,), (1,)), ((), ())), preferred_element_type=jnp.float32
            )
            scores.append(jnp.where(bias < 0.0, NEG_FILL, product))
            jobs.append((u, j, h, query_live))
    tops = [jnp.max(s, axis=1, keepdims=True) for s in scores]
    weights = [jnp.exp2((s - m) * EXP_SCALE) for s, m in zip(scores, tops)]
    totals = [jnp.sum(w, axis=1, keepdims=True) for w in weights]
    for (u, j, h, query_live), w, total in zip(jobs, weights, totals):
        v = line[u, :, 2 * width + h * HD : 2 * width + (h + 1) * HD]
        added = lax.dot_general(
            w.astype(jnp.bfloat16), v, (((1,), (0,)), ((), ())), preferred_element_type=jnp.float32
        )
        safe = jnp.where(query_live, total, 1.0)
        done = jnp.where(query_live, added / safe, 0.0)
        held[h, pl.ds(j, cells, stride=own), :] = done

    @pl.when(step == pl.num_programs(0) - 1)
    def _():
        for s in range(peers):
            at = pl.multiple_of((me ^ s) * span * own, span * own)
            for h in range(HC):
                part = held[h, pl.ds(at, span * own), :].reshape(span, own, HD)
                outs[s][:, :, h * HD : (h + 1) * HD] = part.astype(jnp.bfloat16)


def col_attend(me, pattern, chosen, count, pieces):
    peers = len(pieces)
    own, span, wide = pieces[0].shape
    width = HC * HD
    lines = 2
    result = (span, own, width)
    return pl.pallas_call(
        functools.partial(col_attend_kernel, chosen=chosen, lines=lines),
        grid_spec=pltpu.PrefetchScalarGridSpec(
            num_scalar_prefetch=3,
            grid=(own // lines,),
            in_specs=[pl.BlockSpec(memory_space=pltpu.VMEM)] * peers,
            out_specs=[pl.BlockSpec(result, lambda j, *_: (0, 0, 0))] * peers,
            scratch_shapes=[
                pltpu.VMEM((lines, peers * span, wide), jnp.bfloat16),
                pltpu.VMEM((HC, own * peers * span, HD), jnp.float32),
            ],
        ),
        out_shape=[jax.ShapeDtypeStruct(result, jnp.bfloat16)] * peers,
        compiler_params=grant(56),
        name="col_attend",
    )(me, pattern, count, pieces[0], *[in_place(p) for p in pieces[1:]])


def fetch_weights(plane, weights, line, sem, step, slot, flipped):
    near = weights[0].shape[0]
    at_x, at_z = lax.div(plane, near), lax.rem(plane, near)
    turn = lax.rem(step, near)
    for core in range(2):

        @pl.when(lax.div(step, near) == core)
        def _(core=core):
            for a in range(near):
                for b in range(near):
                    x, z = (b, a) if flipped else (a, b)
                    source = weights[core * near + a].at[b, turn]
                    span = source.shape[0]
                    at = pl.multiple_of(((at_x ^ x) * near + (at_z ^ z)) * span, span)
                    target = line.at[slot, pl.ds(at, span), :]
                    pltpu.make_async_copy(source, target, sem.at[slot]).start()


def project_step(plane, weights, line, sem, flipped, heads):
    step = pl.program_id(0)
    slot = lax.rem(step, 2)

    @pl.when(step == 0)
    def _():
        fetch_weights(plane, weights, line, sem, step, slot, flipped)

    @pl.when(step + 1 < pl.num_programs(0))
    def _():
        fetch_weights(plane, weights, line, sem, step + 1, 1 - slot, flipped)

    pltpu.make_async_copy(line.at[slot], line.at[slot], sem.at[slot]).wait()
    return lax.dot_general(
        heads[...].reshape(-1, heads.shape[2]),
        line[slot],
        (((1,), (1,)), ((), ())),
        preferred_element_type=jnp.float32,
    )


def project_rows_kernel(place, heads, *rest):
    weights, (out_ref, line, sem) = rest[:-3], rest[-3:]
    added = project_step(place[1], weights, line, sem, False, heads)
    out_ref[pl.program_id(0)] = added


def project_cols_kernel(place, *rest, peers):
    pieces, weights = rest[:peers], rest[peers:-5]
    partial_ref, out_ref, heads, line, sem = rest[-5:]
    own = pieces[0].shape[1]

    @pl.when(pl.program_id(0) == 0)
    def _():
        me = place[0]
        odd = lax.rem(me, 2) == 1
        for s in range(0, peers, 2):
            a = pieces[s][...].astype(jnp.float32)
            b = pieces[s + 1][...].astype(jnp.float32)
            both = jnp.concatenate([jnp.where(odd, b, a), jnp.where(odd, a, b)], axis=1)
            at = pl.multiple_of(((me ^ s) // 2) * 2 * own, 2 * own)
            heads[:, pl.ds(at, 2 * own), :] = both.astype(jnp.bfloat16)

    added = project_step(place[1], weights, line, sem, True, heads)
    out_ref[...] = (partial_ref[pl.program_id(0)] + added).astype(jnp.bfloat16)


def project_sizes(weights):
    near, turns, part, width = weights[0].shape
    tile = near * near * part

    def target(j, at):
        return 0, at[0] ^ (2 * lax.rem(j, turns) + lax.div(j, turns))

    scratch = [pltpu.VMEM((2, tile, width), jnp.bfloat16), pltpu.SemaphoreType.DMA((2,))]
    return 2 * turns, tile, target, scratch


def project_rows(place, row_out, weights):
    span, cells, _ = row_out.shape
    steps, tile, _, scratch = project_sizes(weights)
    return pl.pallas_call(
        project_rows_kernel,
        grid_spec=pltpu.PrefetchScalarGridSpec(
            num_scalar_prefetch=1,
            grid=(steps,),
            in_specs=[pl.BlockSpec(memory_space=pltpu.VMEM)]
            + [pl.BlockSpec(memory_space=pl.ANY)] * len(weights),
            out_specs=pl.BlockSpec(memory_space=pltpu.VMEM),
            scratch_shapes=scratch,
        ),
        out_shape=pltpu.VMEM((steps, span * cells, tile), jnp.float32),
        compiler_params=grant(20),
        name="project_rows",
    )(place, in_place(row_out), *weights)


def project_cols(place, pieces, weights, partial, outs):
    span, own, width = pieces[0].shape
    steps, tile, target, scratch = project_sizes(weights)
    held = pl.BlockSpec(memory_space=pltpu.VMEM)
    return pl.pallas_call(
        functools.partial(project_cols_kernel, peers=len(pieces)),
        grid_spec=pltpu.PrefetchScalarGridSpec(
            num_scalar_prefetch=1,
            grid=(steps,),
            in_specs=[held] * len(pieces)
            + [pl.BlockSpec(memory_space=pl.ANY)] * len(weights)
            + [held],
            out_specs=pl.BlockSpec((partial.shape[1], tile), target),
            scratch_shapes=[pltpu.VMEM((span, own * len(pieces), width), jnp.bfloat16)] + scratch,
        ),
        out_shape=jax.ShapeDtypeStruct((partial.shape[1], outs), jnp.bfloat16),
        compiler_params=grant(20),
        name="project_cols",
    )(place, pieces[0], *[in_place(p) for p in pieces[1:]], *weights, in_place(partial))


def by_xor(x, axis, masks):
    size = lax.axis_size(axis)
    return [lax.ppermute(x, axis, [(d, d ^ s) for d in range(size)]) for s in masks]


def swap_pieces(pieces):
    peers = len(pieces)
    return [pieces[0]] + [
        lax.ppermute(pieces[s], "rows", [(d, d ^ s) for d in range(peers)])
        for s in range(1, peers)
    ]


def join_kernel(*refs):
    parts, outs = refs[:-2], refs[-2:]
    each = len(parts) // 2
    for i, part in enumerate(parts):
        outs[i // each][i % each] = part[...]


def join_both(first, second):
    held = pl.BlockSpec(memory_space=pltpu.VMEM)
    whole = jax.ShapeDtypeStruct((len(first),) + first[0].shape, first[0].dtype)
    return pl.pallas_call(
        join_kernel,
        in_specs=[held] * (len(first) + len(second)),
        out_specs=[held, held],
        out_shape=[whole, whole],
        compiler_params=grant(56),
        name="join_both",
    )(
        first[0],
        *[in_place(p) for p in first[1:]],
        second[0],
        *[in_place(p) for p in second[1:]],
    )


def halve_kernel(*refs):
    parts, (upper, lower) = refs[:-4], refs[-2:]
    middle = upper.shape[2]
    for i, part in enumerate(parts):
        upper[i] = part[:, :middle]
        lower[i] = part[:, middle:]


def halve(parts, tables):
    span, channels = parts[0].shape
    half = jax.ShapeDtypeStruct((len(parts), span, channels // 2), parts[0].dtype)
    held = pl.BlockSpec(memory_space=pltpu.VMEM)
    return pl.pallas_call(
        halve_kernel,
        in_specs=[held] * len(parts) + [pl.BlockSpec(memory_space=pl.ANY)] * len(tables),
        out_specs=[held, held],
        out_shape=[half, half],
        compiler_params=grant(56),
        name="halve",
    )(parts[0], *[in_place(p) for p in parts[1:]], *tables)


def body(
    query_cells, key_cells, value_cells, out_weight, row_pattern, row_count, col_pattern, col_count
):
    row_span, col_span, _ = query_cells.shape
    peers = lax.axis_size("rows")
    row_share = row_span // lax.axis_size("cols")
    me = lax.axis_index("rows").astype(jnp.int32).reshape(1)
    row_first = lax.axis_index("cols") * row_share
    chosen = row_pattern.shape[-1]
    pattern = lax.dynamic_slice_in_dim(row_pattern, row_first, row_share, 0).reshape(-1)
    col_listed = col_pattern.reshape(-1)
    count = lax.dynamic_slice_in_dim(row_count, row_first, row_share, 0)

    place = jnp.stack([lax.axis_index("rows"), lax.axis_index("cols")]).astype(jnp.int32)

    shard = out_weight.T
    packed = row_pack(query_cells, key_cells, value_cells)
    lines = lax.all_to_all(packed, "cols", 0, 0, tiled=True)
    along_y = [shard] + by_xor(shard, "rows", (2, 4, 6))
    sent = col_pack(me, query_cells, key_cells, value_cells, peers)
    pieces = swap_pieces(sent)
    upper, lower = halve(along_y, (pattern, col_listed))
    along_z = [upper] + by_xor(upper, "cols", (1, 2, 3))
    along_x = [lower] + by_xor(lower, "cols", (4, 8, 12))
    upper, lower = join_both(along_z, along_x)
    uppers = [upper] + by_xor(upper, "cols", (4, 8, 12))
    lowers = [lower] + by_xor(lower, "cols", (1, 2, 3))
    row_out = row_attend(pattern, chosen, count, lines)
    row_out = lax.all_to_all(row_out.reshape(row_span, col_span, -1), "cols", 0, 0, tiled=True)
    col_out = col_attend(me, col_listed, col_pattern.shape[-1], col_count, pieces)
    col_out = swap_pieces(col_out)
    uppers += [by_xor(w, "rows", (1,))[0] for w in uppers]
    lowers += [by_xor(w, "rows", (1,))[0] for w in lowers]
    outs = out_weight.shape[1] * peers * lax.axis_size("cols")
    partial = project_rows(place, row_out, uppers)
    projected = project_cols(place, col_out, lowers, partial, outs)
    return projected.reshape(row_span, col_span, projected.shape[-1])


def solution(mesh):
    placed = (
        P("rows", "cols", None),
        P("rows", "cols", None),
        P("rows", "cols", None),
        P(None, ("rows", "cols")),
        P("rows", None, None),
        P("rows"),
        P("cols", None, None),
        P("cols"),
    )
    return jax.shard_map(
        body, mesh=mesh, in_specs=placed, out_specs=P("rows", "cols", None), check_vma=False
    )
```

```python
import functools
import math

import jax
import jax.numpy as jnp
from jax import lax
from jax.experimental import pallas as pl
from jax.experimental.pallas import tpu as pltpu
from jax.sharding import PartitionSpec as P


HR = 4
HC = 4
HD = 128
BLK = 32
NEG_FILL = -1e30
UNROLL = 4
EXP_SCALE = HD ** (-0.5) * math.log2(math.e)


def grant(mebibytes):
    return pltpu.CompilerParams(vmem_limit_bytes=mebibytes << 20)


def in_place(x):
    return pltpu.with_memory_space_constraint(x, pltpu.VMEM)


def row_pack_kernel(q_ref, k_ref, v_ref, out_ref):
    width = HR * HD
    out_ref[:, :, 0:width] = q_ref[...]
    out_ref[:, :, width : 2 * width] = k_ref[...]
    out_ref[:, :, 2 * width : 3 * width] = v_ref[...]


def row_pack(q, k, v):
    span, cells, _ = q.shape
    width = HR * HD
    step = 4
    part = pl.BlockSpec((step, cells, width), lambda i: (i, 0, 0))
    return pl.pallas_call(
        row_pack_kernel,
        grid=(span // step,),
        in_specs=[part, part, part],
        out_specs=pl.BlockSpec((step, cells, 3 * width), lambda i: (i, 0, 0)),
        out_shape=jax.ShapeDtypeStruct((span, cells, 3 * width), q.dtype),
        compiler_params=grant(56),
        name="row_pack",
    )(q, k, v)


def col_pack_kernel(me_ref, q_ref, k_ref, v_ref, *rest):
    outs, (wide, buf, sem) = rest[:-3], rest[-3:]
    peers = len(outs)
    width = HC * HD
    span, own, _ = q_ref.shape
    step = pl.program_id(0)
    slot = lax.rem(step, 2)

    @pl.when(step >= 2)
    def _():
        pltpu.make_async_copy(buf.at[slot], outs[0], sem.at[slot]).wait()

    for t, ref in enumerate((q_ref, k_ref, v_ref)):
        for h in range(HC):
            lanes = slice(h * HD, (h + 1) * HD)
            wide[t * HC + h] = ref[:, :, lanes].reshape(span * own, HD).astype(jnp.float32)
    for t in range(3):
        for h in range(HC):
            for j in range(own):
                line = wide[t * HC + h, pl.ds(j, span, stride=own), :]
                at = t * width + h * HD
                buf[slot, j, :, at : at + HD] = line.astype(jnp.bfloat16)
    for s in range(peers):

        @pl.when(step == s)
        def _(s=s):
            pltpu.make_async_copy(buf.at[slot], outs[s], sem.at[slot]).start()

    @pl.when(step == peers - 1)
    def _():
        pltpu.make_async_copy(buf.at[1 - slot], outs[0], sem.at[1 - slot]).wait()
        pltpu.make_async_copy(buf.at[slot], outs[0], sem.at[slot]).wait()


def col_pack(me, q, k, v, peers):
    span, cells, _ = q.shape
    width = HC * HD
    own = cells // peers
    part = pl.BlockSpec((span, own, width), lambda s, me: (0, me[0] ^ s, 1))
    piece = (own, span, 3 * width)
    return pl.pallas_call(
        col_pack_kernel,
        grid_spec=pltpu.PrefetchScalarGridSpec(
            num_scalar_prefetch=1,
            grid=(peers,),
            in_specs=[part, part, part],
            out_specs=[pl.BlockSpec(memory_space=pl.ANY)] * peers,
            scratch_shapes=[
                pltpu.VMEM((3 * HC, span * own, HD), jnp.float32),
                pltpu.VMEM((2,) + piece, q.dtype),
                pltpu.SemaphoreType.DMA((2,)),
            ],
        ),
        out_shape=[jax.ShapeDtypeStruct(piece, q.dtype)] * peers,
        compiler_params=grant(56),
        name="col_pack",
    )(me, q, k, v)


def row_attend_kernel(pattern_ref, count_ref, x_ref, out_ref, *, chosen):
    width = HR * HD
    count = count_ref[0]
    per = x_ref.shape[1] // BLK
    blocks = x_ref.shape[0] * per
    key_lane = lax.broadcasted_iota(jnp.int32, (1, chosen * BLK), 1)
    slot_of = key_lane // BLK
    in_block = key_lane - slot_of * BLK
    query_row = lax.broadcasted_iota(jnp.int32, (BLK, 1), 0)
    zero = jnp.zeros((BLK, HD), jnp.bfloat16)

    def block(b, lanes):
        at = pl.multiple_of(lax.rem(b, per) * BLK, BLK)
        return x_ref[lax.div(b, per), pl.ds(at, BLK), lanes]

    def stage_scores(n):
        q = block(n, slice(0, width))
        keys = []
        limit = jnp.zeros((1, chosen * BLK), jnp.int32)
        for s in range(chosen):
            b = pattern_ref[n * chosen + s]
            keys.append(block(b, slice(width, 2 * width)))
            limit = jnp.where(slot_of == s, count - b * BLK, limit)
        keys = jnp.concatenate(keys, axis=0)
        live = in_block < limit
        spread = jnp.concatenate(
            [
                jnp.concatenate(
                    [q[:, h * HD : (h + 1) * HD] if g == h else zero for g in range(HR)], axis=1
                )
                for h in range(HR)
            ],
            axis=0,
        )
        scores = lax.dot_general(
            spread, keys, (((1,), (1,)), ((), ())), preferred_element_type=jnp.float32
        )
        return jnp.where(live, scores, NEG_FILL)

    def stage_values(n, weights, total):
        at = pl.multiple_of(n * BLK, BLK)
        values = []
        for s in range(chosen):
            values.append(block(pattern_ref[n * chosen + s], slice(2 * width, 3 * width)))
        values = jnp.concatenate(values, axis=0)
        query_live = (query_row + n * BLK) < count
        for pair in range(HR // 2):
            rows = slice(pair * 2 * BLK, (pair + 1) * 2 * BLK)
            lanes = slice(pair * 2 * HD, (pair + 1) * 2 * HD)
            added = lax.dot_general(
                weights[rows],
                values[:, lanes],
                (((1,), (0,)), ((), ())),
                preferred_element_type=jnp.float32,
            )
            for g in range(2):
                h = pair * 2 + g
                part = added[g * BLK : (g + 1) * BLK, g * HD : (g + 1) * HD]
                safe = jnp.where(query_live, total[h * BLK : (h + 1) * BLK], 1.0)
                done = jnp.where(query_live, part / safe, 0.0)
                out_ref[pl.ds(at, BLK), h * HD : (h + 1) * HD] = done.astype(jnp.bfloat16)

    def group(g, _):
        blocks_here = [g * UNROLL + u for u in range(UNROLL)]
        scores = [stage_scores(n) for n in blocks_here]
        tops = [jnp.max(s, axis=1, keepdims=True) for s in scores]
        weights = [jnp.exp2((s - m) * EXP_SCALE) for s, m in zip(scores, tops)]
        totals = [jnp.sum(w, axis=1, keepdims=True) for w in weights]
        for n, w, t in zip(blocks_here, weights, totals):
            stage_values(n, w.astype(jnp.bfloat16), t)
        return 0

    lax.fori_loop(0, blocks // UNROLL, group, 0)


def row_attend(pattern, chosen, count, x):
    cells = x.shape[0] * x.shape[1]
    return pl.pallas_call(
        functools.partial(row_attend_kernel, chosen=chosen),
        grid_spec=pltpu.PrefetchScalarGridSpec(
            num_scalar_prefetch=2,
            grid=(1,),
            in_specs=[pl.BlockSpec(memory_space=pltpu.VMEM)],
            out_specs=pl.BlockSpec((cells, HR * HD), lambda i, *_: (0, 0)),
        ),
        out_shape=jax.ShapeDtypeStruct((cells, HR * HD), x.dtype),
        compiler_params=grant(56),
        name="row_attend",
    )(pattern, count, in_place(x))


def col_attend_kernel(me_ref, pattern_ref, count_ref, *rest, chosen, lines):
    peers = (len(rest) - 2) // 2
    pieces, outs, (line, held) = rest[:peers], rest[peers : 2 * peers], rest[2 * peers :]
    width = HC * HD
    me = me_ref[0]
    step = pl.program_id(0)
    span = pieces[0].shape[1]
    cells = peers * span
    own = held.shape[1] // cells
    blocks = cells // BLK
    key_at = lax.broadcasted_iota(jnp.int32, (1, cells), 1)
    key_block = key_at // BLK
    query_row = lax.broadcasted_iota(jnp.int32, (cells, 1), 0)
    for u in range(lines):
        for s in range(peers):
            line[u, pl.ds(pl.multiple_of((me ^ s) * span, span), span), :] = pieces[s][step * lines + u]
    jobs, scores = [], []
    for u in range(lines):
        j = step * lines + u
        first = me * own + j
        count = count_ref[first]
        rows = []
        for n in range(blocks):
            listed = key_block == pattern_ref[(first * blocks + n) * chosen]
            for s in range(1, chosen):
                listed = listed | (key_block == pattern_ref[(first * blocks + n) * chosen + s])
            row = jnp.where(listed & (key_at < count), 0.0, NEG_FILL)
            rows.append(jnp.broadcast_to(row, (BLK, cells)))
        bias = jnp.concatenate(rows, axis=0)
        query_live = query_row < count
        for h in range(HC):
            q = line[u, :, h * HD : (h + 1) * HD]
            k = line[u, :, width + h * HD : width + (h + 1) * HD]
            product = lax.dot_general(
                q, k, (((1,), (1,)), ((), ())), preferred_element_type=jnp.float32
            )
            scores.append(jnp.where(bias < 0.0, NEG_FILL, product))
            jobs.append((u, j, h, query_live))
    tops = [jnp.max(s, axis=1, keepdims=True) for s in scores]
    weights = [jnp.exp2((s - m) * EXP_SCALE) for s, m in zip(scores, tops)]
    totals = [jnp.sum(w, axis=1, keepdims=True) for w in weights]
    for (u, j, h, query_live), w, total in zip(jobs, weights, totals):
        v = line[u, :, 2 * width + h * HD : 2 * width + (h + 1) * HD]
        added = lax.dot_general(
            w.astype(jnp.bfloat16), v, (((1,), (0,)), ((), ())), preferred_element_type=jnp.float32
        )
        safe = jnp.where(query_live, total, 1.0)
        done = jnp.where(query_live, added / safe, 0.0)
        held[h, pl.ds(j, cells, stride=own), :] = done

    @pl.when(step == pl.num_programs(0) - 1)
    def _():
        for s in range(peers):
            at = pl.multiple_of((me ^ s) * span * own, span * own)
            for h in range(HC):
                part = held[h, pl.ds(at, span * own), :].reshape(span, own, HD)
                outs[s][:, :, h * HD : (h + 1) * HD] = part.astype(jnp.bfloat16)


def col_attend(me, pattern, chosen, count, pieces):
    peers = len(pieces)
    own, span, wide = pieces[0].shape
    width = HC * HD
    lines = 2
    result = (span, own, width)
    return pl.pallas_call(
        functools.partial(col_attend_kernel, chosen=chosen, lines=lines),
        grid_spec=pltpu.PrefetchScalarGridSpec(
            num_scalar_prefetch=3,
            grid=(own // lines,),
            in_specs=[pl.BlockSpec(memory_space=pltpu.VMEM)] * peers,
            out_specs=[pl.BlockSpec(result, lambda j, *_: (0, 0, 0))] * peers,
            scratch_shapes=[
                pltpu.VMEM((lines, peers * span, wide), jnp.bfloat16),
                pltpu.VMEM((HC, own * peers * span, HD), jnp.float32),
            ],
        ),
        out_shape=[jax.ShapeDtypeStruct(result, jnp.bfloat16)] * peers,
        compiler_params=grant(56),
        name="col_attend",
    )(me, pattern, count, pieces[0], *[in_place(p) for p in pieces[1:]])


def project_kernel(place, row_ref, *rest, peers, near):
    pieces, (out_ref, heads, line, sem) = rest[:peers], rest[-4:]
    weights = rest[peers:-4]
    width = HR * HD
    own = pieces[0].shape[1]
    me, plane = place[0], place[1]
    step = pl.program_id(0)
    slot = lax.rem(step, 2)
    at_x, at_z = lax.div(plane, near), lax.rem(plane, near)

    def fetch(step, slot):
        turn = lax.rem(step, near)
        for core in range(2):

            @pl.when(lax.div(step, near) == core)
            def _(core=core):
                group = weights[2 * near * core : 2 * near * (core + 1)]
                for a in range(near):
                    for b in range(near):
                        for half, (x, z) in enumerate(((a, b), (b, a))):
                            source = group[half * near + a].at[b, turn]
                            span, wide = source.shape
                            at = ((at_x ^ x) * near + (at_z ^ z)) * span
                            target = line.at[
                                slot,
                                pl.ds(pl.multiple_of(at, span), span),
                                pl.ds(half * wide, wide),
                            ]
                            pltpu.make_async_copy(source, target, sem.at[slot]).start()

    @pl.when(step == 0)
    def _():
        fetch(step, slot)
        odd = lax.rem(me, 2) == 1
        heads[:, :, 0:width] = row_ref[...]
        for s in range(0, peers, 2):
            a = pieces[s][...].astype(jnp.float32)
            b = pieces[s + 1][...].astype(jnp.float32)
            both = jnp.concatenate([jnp.where(odd, b, a), jnp.where(odd, a, b)], axis=1)
            at = pl.multiple_of(((me ^ s) // 2) * 2 * own, 2 * own)
            heads[:, pl.ds(at, 2 * own), width:] = both.astype(jnp.bfloat16)

    @pl.when(step + 1 < pl.num_programs(0))
    def _():
        fetch(step + 1, 1 - slot)

    pltpu.make_async_copy(line.at[slot], line.at[slot], sem.at[slot]).wait()
    out_ref[...] = lax.dot_general(
        heads[...].reshape(-1, heads.shape[2]),
        line[slot],
        (((1,), (1,)), ((), ())),
        preferred_element_type=jnp.float32,
    ).astype(jnp.bfloat16)


def project(place, row_out, pieces, weights, outs):
    span, cells, _ = row_out.shape
    turns, near, part, wide = weights[0].shape
    channels = 2 * wide
    tile = near * near * part
    held = pl.BlockSpec(memory_space=pltpu.VMEM)

    def target(j, at):
        return 0, at[0] ^ (2 * lax.rem(j, turns) + lax.div(j, turns))

    return pl.pallas_call(
        functools.partial(project_kernel, peers=len(pieces), near=near),
        grid_spec=pltpu.PrefetchScalarGridSpec(
            num_scalar_prefetch=1,
            grid=(2 * turns,),
            in_specs=[held] * (1 + len(pieces))
            + [pl.BlockSpec(memory_space=pl.ANY)] * len(weights),
            out_specs=pl.BlockSpec((span * cells, tile), target),
            scratch_shapes=[
                pltpu.VMEM((span, cells, channels), jnp.bfloat16),
                pltpu.VMEM((2, tile, channels), jnp.bfloat16),
                pltpu.SemaphoreType.DMA((2,)),
            ],
        ),
        out_shape=jax.ShapeDtypeStruct((span * cells, outs), jnp.bfloat16),
        compiler_params=grant(56),
        name="project",
    )(place, in_place(row_out), pieces[0], *[in_place(p) for p in pieces[1:]], *weights)


def by_xor(x, axis, masks):
    size = lax.axis_size(axis)
    return [lax.ppermute(x, axis, [(d, d ^ s) for d in range(size)]) for s in masks]


def swap_pieces(pieces):
    peers = len(pieces)
    return [pieces[0]] + [
        lax.ppermute(pieces[s], "rows", [(d, d ^ s) for d in range(peers)])
        for s in range(1, peers)
    ]


def join_kernel(*refs):
    parts, outs = refs[:-2], refs[-2:]
    each = len(parts) // 2
    for i, part in enumerate(parts):
        outs[i // each][i % each] = part[...]


def join_both(first, second):
    held = pl.BlockSpec(memory_space=pltpu.VMEM)
    whole = jax.ShapeDtypeStruct((len(first),) + first[0].shape, first[0].dtype)
    return pl.pallas_call(
        join_kernel,
        in_specs=[held] * (len(first) + len(second)),
        out_specs=[held, held],
        out_shape=[whole, whole],
        compiler_params=grant(56),
        name="join_both",
    )(
        first[0],
        *[in_place(p) for p in first[1:]],
        second[0],
        *[in_place(p) for p in second[1:]],
    )


def halve_kernel(*refs):
    parts, (upper, lower) = refs[:-6], refs[-2:]
    middle = upper.shape[2]
    for i, part in enumerate(parts):
        upper[i] = part[:, :middle]
        lower[i] = part[:, middle:]


def halve(parts, tables):
    span, channels = parts[0].shape
    half = jax.ShapeDtypeStruct((len(parts), span, channels // 2), parts[0].dtype)
    held = pl.BlockSpec(memory_space=pltpu.VMEM)
    return pl.pallas_call(
        halve_kernel,
        in_specs=[held] * len(parts) + [pl.BlockSpec(memory_space=pl.ANY)] * len(tables),
        out_specs=[held, held],
        out_shape=[half, half],
        compiler_params=grant(56),
        name="halve",
    )(parts[0], *[in_place(p) for p in parts[1:]], *tables)


def body(
    query_cells, key_cells, value_cells, out_weight, row_pattern, row_count, col_pattern, col_count
):
    row_span, col_span, _ = query_cells.shape
    peers = lax.axis_size("rows")
    row_share = row_span // lax.axis_size("cols")
    me = lax.axis_index("rows").astype(jnp.int32).reshape(1)
    row_first = lax.axis_index("cols") * row_share
    chosen = row_pattern.shape[-1]
    pattern = lax.dynamic_slice_in_dim(row_pattern, row_first, row_share, 0).reshape(-1)
    col_listed = col_pattern.reshape(-1)
    count = lax.dynamic_slice_in_dim(row_count, row_first, row_share, 0)

    place = jnp.stack([lax.axis_index("rows"), lax.axis_index("cols")]).astype(jnp.int32)

    shard = out_weight.T
    packed = row_pack(query_cells, key_cells, value_cells)
    lines = lax.all_to_all(packed, "cols", 0, 0, tiled=True)
    along_y = [shard] + by_xor(shard, "rows", (2, 4, 6))
    sent = col_pack(me, query_cells, key_cells, value_cells, peers)
    pieces = swap_pieces(sent)
    upper, lower = halve(along_y, (pattern, col_listed, count, place))
    along_z = [upper] + by_xor(upper, "cols", (1, 2, 3))
    along_x = [lower] + by_xor(lower, "cols", (4, 8, 12))
    upper, lower = join_both(along_z, along_x)
    uppers = [upper] + by_xor(upper, "cols", (4, 8, 12))
    lowers = [lower] + by_xor(lower, "cols", (1, 2, 3))
    row_out = row_attend(pattern, chosen, count, lines)
    row_out = lax.all_to_all(row_out.reshape(row_span, col_span, -1), "cols", 0, 0, tiled=True)
    col_out = col_attend(me, col_listed, col_pattern.shape[-1], col_count, pieces)
    col_out = swap_pieces(col_out)
    uppers += [by_xor(w, "rows", (1,))[0] for w in uppers]
    lowers += [by_xor(w, "rows", (1,))[0] for w in lowers]
    outs = out_weight.shape[1] * peers * lax.axis_size("cols")
    near = len(along_z)
    weights = uppers[:near] + lowers[:near] + uppers[near:] + lowers[near:]
    projected = project(place, row_out, col_out, weights, outs)
    return projected.reshape(row_span, col_span, projected.shape[-1])


def solution(mesh):
    placed = (
        P("rows", "cols", None),
        P("rows", "cols", None),
        P("rows", "cols", None),
        P(None, ("rows", "cols")),
        P("rows", None, None),
        P("rows"),
        P("cols", None, None),
        P("cols"),
    )
    return jax.shard_map(
        body, mesh=mesh, in_specs=placed, out_specs=P("rows", "cols", None), check_vma=False
    )
```
